128 devices in a mesh: gx: 8 (over z, y_hi), gy: 16 (over x, y_lo, core).
Axes of the slice: x: 4, y: 4 (y_hi: 2, y_lo: 2; y = y_hi * 2 + y_lo), z: 4, core: 2. Of those that a mesh axis runs over, the one named last changes fastest.
Arguments:
- interior_inverse: bfloat16 [16, 16, 1536, 1536], P('gx', 'gy'), as said below
- coupling: bfloat16 [16, 16, 1536, 1024], P('gx', 'gy'), may hold values from -0.15625 to 0.15625
- face_stiffness: bfloat16 [16, 16, 4, 256, 256], P('gx', 'gy'), as said below
- corner_basis: bfloat16 [16, 16, 24, 1024], P('gx', 'gy'), may hold values from -0.25 to 0.25
- loads: float32 [16, 16, 4, 256], P('gx', 'gy'), may hold values from -48 to 48
- face_order: int32 [16, 16, 4, 256], P('gx', 'gy'), may hold values from 0 to 255, each once within a row
- corner_index: int32 [16, 16, 24], P('gx', 'gy'), may hold values from 0 to 1791, as said below
- coarse_inverse: float32 [1792, 1792], P(None, ('gx', 'gy')), as said below
Outputs:
- solution: float32 [16, 16, 4, 256], P('gx', 'gy')
- residual: float32 [16, 16, 4, 256], P('gx', 'gy')
The draws below stay inside these ranges and needn't reach their ends.
Inputs may be any that keep to these rules, and one draw needn't show every extreme that they name: `interior_inverse`: symmetric positive definite. `face_stiffness`: each block is symmetric, and every subdomain's interface Schur complement is positive definite. `corner_index`: subdomains that share a grid vertex give its 6 coarse dofs the same indices in the same order (corners in the order top-left, top-right, bottom-left, bottom-right); the 24 indices of a subdomain are distinct; distinct vertices have distinct indices. `coarse_inverse`: symmetric positive definite.
All inputs are finite; a program needn't handle non-finite values.
Results may differ from the reference program's by a relative error of at most 0.01.
Values sent between devices are 32-bit elements; how exact they have to be, the bound alone decides.
No kernel may reach another device: no remote copies, remote signals or barrier semaphores. Data moves between devices by JAX's collectives and lax.ppermute only.
A program may use at most 128 MiB of HBM per device.

```python
import math
import jax
import jax.numpy as jnp
from jax import lax

NI = 1536
NF = 256
NVD = 6
ITERS = 2
NCOR = 24
ROWS = 16
COLS = 16
NCOARSE = 1792


def draw_interior_inverse(key, part):
    first_key, second_key = jax.random.split(key)
    diagonal = jnp.exp(jax.random.uniform(first_key, (ROWS * COLS, NI), jnp.float32, math.log(0.6), math.log(1.2)))
    keys_all = jax.random.split(second_key, ROWS * COLS)

    def one_matrix(items):
        single_key, single_diag = items
        noise = jax.random.normal(single_key, (NI, NI), jnp.float32)
        matrix = (noise + noise.T) * (0.22 / math.sqrt(2.0 * NI)) + jnp.diag(single_diag)
        return matrix.astype(jnp.bfloat16)
    return lax.map(one_matrix, (keys_all, diagonal)).reshape(ROWS, COLS, NI, NI)


def draw_face_stiffness(key, part):
    count_all = ROWS * COLS * 4
    keys_all = jax.random.split(jax.random.fold_in(key, 11), count_all)

    def one_block(single_key):
        factor = jax.random.normal(single_key, (NF, NF), jnp.float32)
        product = jnp.dot(factor, factor.T, precision=lax.Precision.HIGHEST) * (4.0 / NF)
        matrix = 0.5 * (product + product.T) + 8.0 * jnp.eye(NF, dtype=jnp.float32)
        return matrix.astype(jnp.bfloat16)
    return lax.map(one_block, keys_all).reshape(ROWS, COLS, 4, NF, NF)


def draw_corner_index(key, part):
    vertex_dofs = (ROWS + 1) * (COLS + 1) * NVD
    shuffled = jax.random.permutation(jax.random.fold_in(key, 7), NCOARSE).astype(jnp.int32)
    table = shuffled[:vertex_dofs].reshape(ROWS + 1, COLS + 1, NVD)
    corners = jnp.stack([table[:-1, :-1], table[:-1, 1:], table[1:, :-1], table[1:, 1:]], axis=2)
    return corners.reshape(ROWS, COLS, 4 * NVD).astype(jnp.int32)


def draw_coarse_inverse(key, part):
    first_key, second_key = jax.random.split(key)
    diagonal = jnp.exp(jax.random.uniform(first_key, (NCOARSE,), jnp.float32, math.log(0.5), math.log(2.0)))
    noise = jax.random.normal(second_key, (NCOARSE, NCOARSE), jnp.float32)
    matrix = (noise + noise.T) * (0.1 / math.sqrt(NCOARSE)) + jnp.diag(diagonal)
    return matrix.astype(jnp.float32)


def levels(key, dims, pieces, low, largest):
    def one(position, parts):
        heights = jax.random.uniform(jax.random.fold_in(jax.random.fold_in(key, 6), position), (parts,), jnp.float32, low / len(pieces), largest / len(pieces))
        return jnp.repeat(jnp.exp(heights), dims[position] // parts).reshape((-1,) + (1,) * (len(dims) - position - 1))

    gain = one(*pieces[0])
    for cut in pieces[1:]:
        gain = gain * one(*cut)
    return gain


def bell_draw(own_key, extent, width, limit, shards=(), kind=jnp.bfloat16):
    values = width * jax.random.normal(own_key, extent, jnp.float32)
    if shards:
        values = values * levels(own_key, extent, shards, -0.22, 0.18)
    return jnp.clip(values, -limit, limit).astype(kind)


def setup_inputs(seed: int = 0) -> dict:
    seeds = jax.random.split(jax.random.key(seed), 9)
    interior_inverse = draw_interior_inverse(jax.random.fold_in(seeds[8], 71), 0)
    coupling = bell_draw(seeds[1], (ROWS, COLS, NI, 4 * NF), NI ** -0.5, 0.15625, ((0, 8), (1, 16)))
    face_stiffness = draw_face_stiffness(jax.random.fold_in(seeds[8], 71), 0)
    corner_basis = bell_draw(seeds[3], (ROWS, COLS, NCOR, 4 * NF), (2 * NF) ** -0.5, 0.25, ((0, 8), (1, 16)))
    loads = bell_draw(seeds[4], (ROWS, COLS, 4, NF), 8.0, 48.0, ((0, 8), (1, 16)), jnp.float32)
    face_order = jax.vmap(lambda own: jax.random.permutation(own, NF))(jax.random.split(seeds[5], ROWS * COLS * 4)).reshape((ROWS, COLS, 4, NF)).astype(jnp.int32)
    corner_index = draw_corner_index(jax.random.fold_in(seeds[8], 71), 0)
    coarse_inverse = draw_coarse_inverse(jax.random.fold_in(seeds[8], 71), 0)
    return {"interior_inverse": interior_inverse, "coupling": coupling, "face_stiffness": face_stiffness, "corner_basis": corner_basis, "loads": loads, "face_order": face_order, "corner_index": corner_index, "coarse_inverse": coarse_inverse}


careful = lax.Precision.HIGHEST

def opposite(values):
    zero_rows = jnp.zeros_like(values[:1, :, 0])
    zero_cols = jnp.zeros_like(values[:, :1, 0])
    north_side = jnp.concatenate([zero_rows, values[:-1, :, 1]], axis=0)
    south_side = jnp.concatenate([values[1:, :, 0], zero_rows], axis=0)
    west_side = jnp.concatenate([zero_cols, values[:, :-1, 3]], axis=1)
    east_side = jnp.concatenate([values[:, 1:, 2], zero_cols], axis=1)
    return jnp.stack([north_side, south_side, west_side, east_side], axis=2)

def reorder(values, positions):
    return jnp.take_along_axis(values, positions, axis=-1)

def reorder_block(matrix, positions):
    row_pick = jnp.take_along_axis(matrix, jnp.broadcast_to(positions[..., :, None], matrix.shape), axis=-2)
    return jnp.take_along_axis(row_pick, jnp.broadcast_to(positions[..., None, :], matrix.shape), axis=-1)

def invert(summed):
    factor_low = jnp.linalg.cholesky(summed)
    identity = jnp.broadcast_to(jnp.eye(summed.shape[-1], dtype=jnp.float32), summed.shape)
    factor = lax.linalg.triangular_solve(factor_low, identity, left_side=True, lower=True)
    return jnp.einsum('...ik,...il->...kl', factor, factor, precision=careful)

def half_inner(first, second):
    return 0.5 * jnp.sum(first * second)

def reference(interior_inverse, coupling, face_stiffness, corner_basis, loads, face_order, corner_index, coarse_inverse):
    backward = jnp.argsort(face_order, axis=-1).astype(jnp.int32)
    row_ids = jnp.arange(ROWS, dtype=jnp.int32)[:, None] + jnp.zeros((1, COLS), jnp.int32)
    col_ids = jnp.arange(COLS, dtype=jnp.int32)[None, :] + jnp.zeros((ROWS, 1), jnp.int32)
    live_mask = jnp.stack([row_ids > 0, row_ids < ROWS - 1, col_ids > 0, col_ids < COLS - 1], axis=2).astype(jnp.float32)[..., None]
    count_all = ROWS * COLS
    flat_inverse = interior_inverse.reshape(count_all, NI, NI)
    flat_couple = coupling.reshape(count_all, NI, 4 * NF)
    flat_stiff = face_stiffness.reshape(count_all, 4, NF, NF)

    def face_schur(items):
        inverse_mat, couple, stiffness = items
        products = jnp.dot(inverse_mat.astype(jnp.float32), couple.astype(jnp.float32), preferred_element_type=jnp.float32).astype(jnp.bfloat16)
        couple_faces = couple.astype(jnp.float32).reshape(NI, 4, NF)
        product_faces = products.astype(jnp.float32).reshape(NI, 4, NF)
        return stiffness.astype(jnp.float32) - jnp.einsum('ifk,ifl->fkl', couple_faces, product_faces)
    schur_local = lax.map(face_schur, (flat_inverse, flat_couple, flat_stiff)).reshape(ROWS, COLS, 4, NF, NF)
    schur_canon = reorder_block(schur_local, backward)
    face_inverse = invert(schur_canon + opposite(schur_canon))

    def operator(vector_in):
        plain = reorder(vector_in, face_order).astype(jnp.bfloat16).reshape(count_all, 4, NF)

        def one_apply(items):
            inverse_mat, couple, stiffness, values = items
            middle = jnp.dot(couple.astype(jnp.float32), values.reshape(4 * NF).astype(jnp.float32), preferred_element_type=jnp.float32).astype(jnp.bfloat16)
            solved = jnp.dot(inverse_mat.astype(jnp.float32), middle.astype(jnp.float32), preferred_element_type=jnp.float32).astype(jnp.bfloat16)
            direct = jnp.einsum('fkl,fl->fk', stiffness.astype(jnp.float32), values.astype(jnp.float32))
            back_part = jnp.einsum('ifk,i->fk', couple.astype(jnp.float32).reshape(NI, 4, NF), solved.astype(jnp.float32))
            return direct - back_part
        local_out = lax.map(one_apply, (flat_inverse, flat_couple, flat_stiff, plain)).reshape(ROWS, COLS, 4, NF)
        canon_out = reorder(local_out, backward)
        return live_mask * (canon_out + opposite(canon_out))

    def precondition(resid):
        smoothed = jnp.einsum('rcfkl,rcfl->rcfk', face_inverse, resid, precision=careful)
        share = jnp.einsum('rcfkl,rcfl->rcfk', schur_canon, smoothed, precision=careful)
        share_local = reorder(share, face_order).astype(jnp.bfloat16).reshape(ROWS, COLS, 4 * NF)
        corner_res = jnp.einsum('rcjk,rck->rcj', corner_basis.astype(jnp.float32), share_local.astype(jnp.float32))
        coarse_res = jnp.zeros((NCOARSE,), jnp.float32).at[corner_index.reshape(-1)].add(corner_res.reshape(-1))
        coarse_sol = jnp.dot(coarse_inverse, coarse_res, precision=careful)
        corner_sol = coarse_sol[corner_index]
        lifted = jnp.einsum('rcjk,rcj->rck', corner_basis.astype(jnp.float32), corner_sol, precision=careful).reshape(ROWS, COLS, 4, NF)
        spread = jnp.einsum('rcfkl,rcfl->rcfk', schur_canon, reorder(lifted, backward), precision=careful)
        return live_mask * jnp.einsum('rcfkl,rcfl->rcfk', face_inverse, resid + spread + opposite(spread), precision=careful)
    loads_canon = reorder(loads, backward)
    residual = live_mask * (loads_canon + opposite(loads_canon))
    solution = jnp.zeros_like(residual)
    precond_out = precondition(residual)
    gamma = half_inner(residual, precond_out)
    search = precond_out
    for iteration in range(ITERS):
        image = operator(search)
        alpha = gamma / half_inner(search, image)
        solution = solution + alpha * search
        residual = residual - alpha * image
        if iteration + 1 < ITERS:
            precond_out = precondition(residual)
            gamma_next = half_inner(residual, precond_out)
            search = precond_out + gamma_next / gamma * search
            gamma = gamma_next
    return (solution, residual)
```

```python
import jax
import jax.numpy as jnp
from jax import lax
from jax.experimental import pallas as pl
from jax.experimental.pallas import tpu as pltpu
from jax.sharding import Mesh
from jax.sharding import PartitionSpec as P

GX = ("gx_0", "gx_1")
GY = ("gy_0", "gy_1", "gy_2")
GX_GY = GX + GY

NI = 1536
NF = 256
NCOR = 24
NCOARSE = 1792
OWN = 14
GRID_X = 8
GRID_Y = 16
DEV = 128
PKT = 288
STEPS = 3
CHUNK = NI // STEPS
VC = 24
F32 = jnp.float32
BF16 = jnp.bfloat16
HIGHEST = lax.Precision.HIGHEST

FACE = ((0, 1, 3, 5), (1, 2, 4, 6))
GROUPS = ((0, 2), (0, 1), (1, 3), (0, 4), (1, 5), (0, 6), (1, 7))
GROUP_ROW = (0, 1, -1, 2, 0, 1, 0, 1)
GROUP_COL = (1, 1, 1, 1, 0, 0, 2, 2)


def nn(a, b):
    return lax.dot_general(a, b, (((1,), (0,)), ((), ())), preferred_element_type=F32)


def nt(a, b):
    return lax.dot_general(a, b, (((1,), (1,)), ((), ())), preferred_element_type=F32)


def split2(x):
    hi = x.astype(BF16)
    return hi, (x - hi.astype(F32)).astype(BF16)


def split3(x):
    hi = x.astype(BF16)
    rest = x - hi.astype(F32)
    mid = rest.astype(BF16)
    return hi, mid, (rest - mid.astype(F32)).astype(BF16)


def iota(shape, dim):
    return lax.broadcasted_iota(jnp.int32, shape, dim)


def schur_kernel(order, inverse, couple, stiff, basis, loads, index, s_out, p_in, p_n, p_s, p_w, p_e, ct, prod, pick):
    sub = pl.program_id(0)
    step = pl.program_id(1)

    @pl.when(step == 0)
    def _():
        for f in range(4):
            chosen = (iota((NF, NF), 0) == order[f : f + 1, :]).astype(BF16)
            pick[f] = chosen
            ct[f * NF : (f + 1) * NF, :] = nt(chosen, couple[:, f * NF : (f + 1) * NF]).astype(BF16)

    prod[pl.ds(step * CHUNK, CHUNK), :] = nt(inverse[...], ct[...]).astype(BF16)

    @pl.when(step == STEPS - 1)
    def _():
        for f in range(4):
            rows = slice(f * NF, (f + 1) * NF)
            back = nn(ct[rows, :], prod[:, f * NF :])
            chosen = pick[f]
            canon = nt(nn(chosen, stiff[f]).astype(BF16), chosen)
            diag = canon - back[:, :NF]
            s_out[rows, rows] = diag
            if f < 3:
                s_out[rows, (f + 1) * NF :] = -back[:, NF:]
            lowered = nt(basis[:, f * NF : (f + 1) * NF], chosen).astype(BF16)
            hi, lo = split2(diag)
            corner = nn(lowered, hi) + nn(lowered, lo)
            parts = jnp.concatenate(
                [part.astype(F32) for part in split3(jnp.broadcast_to(loads[f : f + 1, :], (8, NF)))], axis=0
            ).astype(BF16)
            placed = nt(parts, chosen)
            load = placed[0:8] + placed[8:16] + placed[16:24]
            tail = jnp.where(iota((8, NF), 0) == 0, load, jnp.broadcast_to(index[...], (8, NF)))

            def put(out, lead):
                out[lead + (slice(0, NF), slice(None))] = diag
                out[lead + (slice(NF, NF + NCOR), slice(None))] = corner
                out[lead + (slice(NF + NCOR, NF + NCOR + 8), slice(None))] = tail

            if f == 0:
                pl.when(sub == 0)(lambda: put(p_n, ()))
                pl.when(sub == 1)(lambda: put(p_in, (1,)))
            elif f == 1:
                pl.when(sub == 0)(lambda: put(p_in, (0,)))
                pl.when(sub == 1)(lambda: put(p_s, ()))
            elif f == 2:
                put(p_w, ())
            else:
                put(p_e, ())


def schur(order, inverse, couple, stiff, basis, loads, index):
    pkt = jax.ShapeDtypeStruct((PKT, NF), F32)
    pair = jax.ShapeDtypeStruct((2, PKT, NF), F32)
    return pl.pallas_call(
        schur_kernel,
        grid=(2, STEPS),
        in_specs=[
            pl.BlockSpec((None, None, 4, NF), lambda s, j: (s, 0, 0, 0)),
            pl.BlockSpec((None, None, CHUNK, NI), lambda s, j: (s, 0, j, 0)),
            pl.BlockSpec((None, None, NI, 4 * NF), lambda s, j: (s, 0, 0, 0)),
            pl.BlockSpec((None, None, 4, NF, NF), lambda s, j: (s, 0, 0, 0, 0)),
            pl.BlockSpec((None, None, NCOR, 4 * NF), lambda s, j: (s, 0, 0, 0)),
            pl.BlockSpec((None, None, 4, NF), lambda s, j: (s, 0, 0, 0)),
            pl.BlockSpec((None, 1, NF), lambda s, j: (s, 0, 0)),
        ],
        out_specs=[
            pl.BlockSpec((None, 4 * NF, 4 * NF), lambda s, j: (s, 0, 0)),
            pl.BlockSpec((2, PKT, NF), lambda s, j: (0, 0, 0)),
            pl.BlockSpec((PKT, NF), lambda s, j: (0, 0)),
            pl.BlockSpec((PKT, NF), lambda s, j: (0, 0)),
            pl.BlockSpec((None, PKT, NF), lambda s, j: (s, 0, 0)),
            pl.BlockSpec((None, PKT, NF), lambda s, j: (s, 0, 0)),
        ],
        out_shape=[jax.ShapeDtypeStruct((2, 4 * NF, 4 * NF), F32), pair, pkt, pkt, pair, pair],
        scratch_shapes=[
            pltpu.VMEM((4 * NF, NI), BF16),
            pltpu.VMEM((NI, 4 * NF), BF16),
            pltpu.VMEM((4, NF, NF), BF16),
        ],
        compiler_params=pltpu.CompilerParams(
            dimension_semantics=("arbitrary", "arbitrary"), vmem_limit_bytes=56 * 2**20
        ),
        cost_estimate=pl.CostEstimate(flops=16 * 10**9, transcendentals=0, bytes_accessed=32 * 2**20),
        name="schur",
    )(order, inverse, couple, stiff, basis, loads, index)


def vertex_kernel(table, columns, out):
    total = jnp.zeros((GRID_Y, 2, 128), F32)
    for ix in range(GRID_X):
        total = total + table[ix * GRID_Y : (ix + 1) * GRID_Y]
    hi, mid, lo = split3(columns[...])
    lhs = jnp.concatenate([hi, mid, lo], axis=0)
    rows = iota((NCOARSE, 256), 0) + 1
    last = total[GRID_Y - 1, 1:2, :]
    for pair in range(9):
        first = total[2 * pair, 0:1, :] if pair < 8 else last
        second = total[2 * pair + 1, 0:1, :] if pair < 8 else jnp.zeros((1, 128), F32)
        wanted = jnp.concatenate([first, second], axis=1).astype(jnp.int32)
        chosen = (rows == wanted).astype(BF16)
        got = nn(lhs, chosen)
        got = got[0:16] + got[16:32] + got[32:48]
        out[2 * pair + 1] = got[:, :128]
        if pair < 8:
            out[2 * pair + 2] = got[:, 128:]
    for other in (0, *range(18, VC)):
        out[other] = jnp.zeros((16, 128), F32)


def vertex_order(table, columns):
    return pl.pallas_call(
        vertex_kernel,
        out_shape=jax.ShapeDtypeStruct((VC, 16, 128), F32),
        compiler_params=pltpu.CompilerParams(vmem_limit_bytes=40 * 2**20),
        cost_estimate=pl.CostEstimate(flops=10**9, transcendentals=0, bytes_accessed=2**20),
        name="vertex_order",
    )(table, columns)


def spread_window(place, contributions):
    corner = iota((NCOR, 128), 0)
    lane = iota((NCOR, 128), 1)
    below = jnp.where(corner >= 12, 1, 0)
    inside = corner - 12 * below
    right = inside >= 6
    dof = inside - jnp.where(right, 6, 0)
    cols = [jnp.zeros((1, 128), F32) for _ in range(4)]
    for g, value in contributions.items():
        target = (2 * place[0] + GROUP_ROW[g] + below) * 6 + dof
        filled = jnp.where(lane == target, jnp.broadcast_to(value, (NCOR, 128)), 0.0)
        left = jnp.sum(jnp.where(right, 0.0, filled), axis=0, keepdims=True)
        both = jnp.sum(filled, axis=0, keepdims=True)
        cols[GROUP_COL[g]] = cols[GROUP_COL[g]] + left
        cols[GROUP_COL[g] + 1] = cols[GROUP_COL[g] + 1] + (both - left)
    return cols


def row_dot(matrix, row):
    return jnp.sum(matrix * row, axis=1, keepdims=True)


def face_kernel(place, live, p_in, p_n, p_s, p_w, p_e, q_n, q_s, q_w, q_e, finv, tmap, r_out, z_out, slots, send, a_hi, a_lo, x):
    def pieces(m):
        if m == 0:
            return p_n, (), q_n, (), live[0]
        if m == 1:
            return p_in, (0,), p_in, (1,), 1.0
        if m == 2:
            return p_s, (), q_s, (), live[1]
        if m < 5:
            return p_w, (m - 3,), q_w, (m - 3,), live[2]
        return p_e, (m - 5,), q_e, (m - 5,), live[3]

    eye = jnp.where(iota((NF, NF), 0) == iota((NF, NF), 1), 1.0, 0.0)
    guess = []
    for m in range(7):
        own, at, other, there, _ = pieces(m)
        full = own[at + (slice(0, NF), slice(None))] + other[there + (slice(0, NF), slice(None))]
        hi, lo = split2(full)
        a_hi[m] = hi
        a_lo[m] = lo
        size = jnp.max(jnp.sum(jnp.abs(full), axis=0, keepdims=True))
        scale = 1.9 / size
        guess.append(scale)
        x[m] = scale * (2.0 * eye - scale * full)

    def rough(state):
        count, _ = state
        worst = jnp.float32(0.0)
        for m in range(7):
            now = x[m]
            near = now.astype(BF16)
            left = eye - nn(a_hi[m], near)
            worst = jnp.maximum(worst, jnp.sum(left * left))
            x[m] = now + nn(near, left.astype(BF16))
        return count + 1, worst

    def rough_on(state):
        count, worst = state
        return jnp.logical_and(count < 24, jnp.logical_not(worst < 0.1))

    _, worst = lax.while_loop(rough_on, rough, (jnp.int32(0), jnp.float32(1e9)))
    fine_start = worst < 0.1

    @pl.when(jnp.logical_not(fine_start))
    def _():
        for m in range(7):
            x[m] = guess[m] * eye

    def fine(state):
        count, _ = state
        worst = jnp.float32(0.0)
        for m in range(7):
            now = x[m]
            hi, lo = split2(now)
            left = eye - (nn(a_hi[m], hi) + (nn(a_hi[m], lo) + nn(a_lo[m], hi)))
            worst = jnp.maximum(worst, jnp.sum(left * left))
            x[m] = now + nn(hi, left.astype(BF16))
        return count + 1, worst

    def fine_on(state):
        count, worst = state
        return jnp.logical_and(count < 60, jnp.logical_not(worst < 1e-4))

    lax.while_loop(fine_on, fine, (jnp.int32(0), jnp.float32(1e9)))

    gathered = {}

    def gather(g, value):
        gathered[g] = value if g not in gathered else gathered[g] + value

    rows_r = []
    rows_z = []
    rows_i = [None] * 8
    for m in range(7):
        own, at, other, there, alive = pieces(m)
        inverse = x[m] * alive
        finv[m] = inverse
        both = jnp.concatenate(
            [own[at + (slice(NF, NF + NCOR), slice(None))], other[there + (slice(NF, NF + NCOR), slice(None))]], axis=0
        )
        b_hi, b_lo = split2(both)
        i_hi, i_lo = split2(inverse)
        lifted = nn(jnp.concatenate([b_hi, b_lo], axis=0), i_hi)
        mapped = lifted[:48] + lifted[48:] + nn(b_hi, i_lo)
        tmap[m] = mapped
        line = slice(NF + NCOR, NF + NCOR + 1)
        resid = alive * (own[at + (line, slice(None))] + other[there + (line, slice(None))])
        rows_r.append(resid)
        resid_hi, resid_mid, resid_lo = split3(jnp.broadcast_to(resid, (8, NF)))
        rows_z.append(resid)
        gather(GROUPS[m][0], row_dot(mapped[:NCOR], resid))
        if m == 1:
            gather(GROUPS[m][1], row_dot(mapped[NCOR:], resid))
        tail = slice(NF + NCOR + 1, NF + NCOR + 2)
        rows_i[GROUPS[m][0]] = own[at + (tail, slice(0, 128))]
        rows_i[GROUPS[m][1]] = other[there + (tail, slice(0, 128))]
    resid = jnp.concatenate(rows_r + [jnp.zeros((1, NF), F32)], axis=0)
    r_out[...] = resid
    z_out[...] = face_apply(finv, resid)
    slots[...] = jnp.transpose(jnp.concatenate(rows_i, axis=0))[:NCOR, :]
    window = jnp.concatenate(spread_window(place, gathered), axis=0)
    send[...] = jnp.broadcast_to(window[None], (DEV, 4, 128))


def face_apply(finv, rows):
    turned = jnp.transpose(rows)
    outs = [jnp.sum(finv[m] * turned[:, m : m + 1], axis=0, keepdims=True) for m in range(7)]
    return jnp.concatenate(outs + [jnp.zeros((1, NF), F32)], axis=0)


def smem():
    return pl.BlockSpec(memory_space=pltpu.SMEM)


def vmem():
    return pl.BlockSpec(memory_space=pltpu.VMEM)


def faces(place, live, *packets):
    return pl.pallas_call(
        face_kernel,
        in_specs=[smem(), smem()] + [vmem()] * 9,
        out_shape=[
            jax.ShapeDtypeStruct((7, NF, NF), F32),
            jax.ShapeDtypeStruct((7, 48, NF), F32),
            jax.ShapeDtypeStruct((8, NF), F32),
            jax.ShapeDtypeStruct((8, NF), F32),
            jax.ShapeDtypeStruct((NCOR, 8), F32),
            jax.ShapeDtypeStruct((DEV, 4, 128), F32),
        ],
        scratch_shapes=[
            pltpu.VMEM((7, NF, NF), BF16),
            pltpu.VMEM((7, NF, NF), BF16),
            pltpu.VMEM((7, NF, NF), F32),
        ],
        compiler_params=pltpu.CompilerParams(vmem_limit_bytes=40 * 2**20),
        cost_estimate=pl.CostEstimate(flops=5 * 10**9, transcendentals=0, bytes_accessed=10 * 2**20),
        name="faces",
    )(place, live, *packets)


def owner_kernel(got, inverse, out, sums, grid):
    grid[...] = jnp.zeros((VC, 128), F32)
    total = jnp.zeros((1, 128), F32)
    for iy in range(GRID_Y):
        part = got[iy, 0:4, :]
        for ix in range(1, GRID_X):
            part = part + got[ix * GRID_Y + iy, 0:4, :]
        grid[iy : iy + 4, :] = grid[iy : iy + 4, :] + part
        total = total + part[0:1, :]
    sums[...] = jnp.broadcast_to(total, (8, 128))
    partial = jnp.zeros((16, 128), F32)
    for col in range(1, 18):
        partial = partial + inverse[col] * grid[col : col + 1, :]
    column = jnp.sum(partial, axis=1, keepdims=True)
    line = jnp.sum(jnp.where(iota((16, 128), 0) == iota((16, 128), 1), column, 0.0), axis=0, keepdims=True)
    out[...] = jnp.broadcast_to(line, (DEV, 128))


def owners(got, inverse):
    return pl.pallas_call(
        owner_kernel,
        out_shape=[jax.ShapeDtypeStruct((DEV, 128), F32), jax.ShapeDtypeStruct((8, 128), F32)],
        scratch_shapes=[pltpu.VMEM((VC, 128), F32)],
        cost_estimate=pl.CostEstimate(flops=10**6, transcendentals=0, bytes_accessed=2**20),
        name="owners",
    )(got, inverse)


def coarse_values(slots, coarse):
    lane = iota((NCOR, 128), 1).astype(F32)
    owner_rows = []
    places = []
    for g in range(8):
        number = slots[:, g : g + 1]
        owner = jnp.floor((number + 0.5) * (1.0 / OWN))
        places.append(number - OWN * owner)
        owner_rows.append(jnp.where(lane == owner, 1.0, 0.0))
    picked = lax.dot_general(
        jnp.concatenate(owner_rows, axis=0),
        coarse[...],
        (((1,), (0,)), ((), ())),
        precision=HIGHEST,
        preferred_element_type=F32,
    )
    return [
        jnp.sum(jnp.where(lane == places[g], picked[g * NCOR : (g + 1) * NCOR], 0.0), axis=1, keepdims=True)
        for g in range(8)
    ]


def prolong(tmap, values):
    outs = []
    for m in range(7):
        column = jnp.concatenate([values[GROUPS[m][0]], values[GROUPS[m][1]]], axis=0)
        outs.append(jnp.sum(tmap[m] * column, axis=0, keepdims=True))
    return jnp.concatenate(outs + [jnp.zeros((1, NF), F32)], axis=0)


def subdomain_apply(s_ref, vector):
    turned = jnp.transpose(vector)
    rows = []
    for s in range(2):
        across = [None] * 4
        upright = [None] * 4
        for f in range(4):
            column = turned[:, FACE[s][f] : FACE[s][f] + 1]
            for g in range(f, 4):
                block = s_ref[s, f * NF : (f + 1) * NF, g * NF : (g + 1) * NF]
                down = jnp.sum(block * column, axis=0, keepdims=True)
                across[g] = down if across[g] is None else across[g] + down
                if g > f:
                    m = FACE[s][g]
                    side = row_dot(block, vector[m : m + 1, :])
                    upright[f] = side if upright[f] is None else upright[f] + side
        columns = jnp.concatenate(
            [jnp.broadcast_to(upright[f], (NF, 128)) if f < 3 else jnp.zeros((NF, 128), F32) for f in range(4)], axis=1
        )
        lane_pick = jnp.concatenate([columns[:, f * 128 : f * 128 + 1] for f in range(4)] * 2, axis=1)
        flipped = jnp.transpose(lane_pick)
        for f in range(4):
            rows.append(across[f] + flipped[f : f + 1, :])
    return jnp.concatenate(rows, axis=0)


def restrict(place, tmap, image):
    gathered = {}

    def gather(g, value):
        gathered[g] = value if g not in gathered else gathered[g] + value

    for m in range(7):
        line = None
        for s in range(2):
            for f in range(4):
                if FACE[s][f] == m:
                    row = image[s * 4 + f : s * 4 + f + 1, :]
                    line = row if line is None else line + row
        gather(GROUPS[m][0], row_dot(tmap[m, 0:NCOR], line))
        gather(GROUPS[m][1], row_dot(tmap[m, NCOR:], line))
    return spread_window(place, gathered)


def post(place, live, image, send):
    me = place[0] * GRID_Y + place[1]

    def put(target, slot, row):
        send[target, slot : slot + 1, :] = image[row : row + 1, 0:128]
        send[target, slot + 1 : slot + 2, :] = image[row : row + 1, 128:256]

    @pl.when(live[0] > 0.0)
    def _():
        put(me - GRID_Y, 4, 0)

    @pl.when(live[1] > 0.0)
    def _():
        put(me + GRID_Y, 4, 5)

    @pl.when(live[2] > 0.0)
    def _():
        put(me - 1, 4, 2)
        put(me - 1, 6, 6)

    @pl.when(live[3] > 0.0)
    def _():
        put(me + 1, 4, 3)
        put(me + 1, 6, 7)


def meet(place, live, image, got):
    me = place[0] * GRID_Y + place[1]

    def read(source, slot, alive):
        at = jnp.clip(source, 0, DEV - 1)
        row = jnp.concatenate([got[at, slot : slot + 1, :], got[at, slot + 1 : slot + 2, :]], axis=1)
        return jnp.where(alive > 0.0, row, 0.0)

    def mine(row):
        return image[row : row + 1, :]

    return jnp.concatenate(
        [
            live[0] * (mine(0) + read(me - GRID_Y, 4, live[0])),
            mine(1) + mine(4),
            live[1] * (mine(5) + read(me + GRID_Y, 4, live[1])),
            live[2] * (mine(2) + read(me - 1, 4, live[2])),
            live[2] * (mine(6) + read(me - 1, 6, live[2])),
            live[3] * (mine(3) + read(me + 1, 4, live[3])),
            live[3] * (mine(7) + read(me + 1, 6, live[3])),
            jnp.zeros((1, NF), F32),
        ],
        axis=0,
    )


def shared_dot(first, second):
    weight = jnp.where(iota((8, NF), 0) == 1, 1.0, 0.5)
    return jnp.sum(weight * first * second)


def sides(vector):
    return jnp.concatenate([vector[m : m + 1, :] for s in range(2) for m in FACE[s]], axis=0)


def tag(row, *scalars):
    lane = iota((1, 128), 1)
    for at, value in scalars:
        row = jnp.where(lane == at, value, row)
    return row


def first_kernel(place, live, s_ref, tmap, resid, smooth, slots, coarse, z_out, c_out, send):
    z = smooth[...] + prolong(tmap, coarse_values(slots, coarse))
    z_out[...] = z
    image = subdomain_apply(s_ref, z)
    c_out[...] = image
    cols = restrict(place, tmap, image)
    gamma = shared_dot(resid[...], z)
    delta = jnp.sum(sides(z) * image)
    cols[0] = tag(cols[0], (120, gamma), (121, delta))
    window = jnp.concatenate(cols + [jnp.zeros((4, 128), F32)], axis=0)
    send[...] = jnp.broadcast_to(window[None], (DEV, 8, 128))
    post(place, live, image, send)


def first(place, live, *rest):
    return pl.pallas_call(
        first_kernel,
        in_specs=[smem(), smem()] + [vmem()] * 6,
        out_shape=[
            jax.ShapeDtypeStruct((8, NF), F32),
            jax.ShapeDtypeStruct((8, NF), F32),
            jax.ShapeDtypeStruct((DEV, 8, 128), F32),
        ],
        compiler_params=pltpu.CompilerParams(vmem_limit_bytes=40 * 2**20),
        cost_estimate=pl.CostEstimate(flops=10**7, transcendentals=0, bytes_accessed=10 * 2**20),
        name="first",
    )(place, live, *rest)


def pick_lane(row, at):
    return jnp.sum(jnp.where(iota((1, 128), 1) == at, row, 0.0))


def second_kernel(place, live, s_ref, finv, tmap, resid, z_old, c_old, slots, coarse, sums, got, z_out, c_out, w_out, r_out, send):
    gamma = pick_lane(sums[0:1, :], 120)
    delta = pick_lane(sums[0:1, :], 121)
    alpha = gamma / delta
    w = meet(place, live, c_old, got)
    w_out[...] = w
    y = face_apply(finv, w) + prolong(tmap, coarse_values(slots, coarse))
    z = z_old[...] - alpha * y
    r = resid[...] - alpha * w
    z_out[...] = z
    r_out[...] = r
    image = subdomain_apply(s_ref, z)
    c_out[...] = image
    gamma_new = shared_dot(r, z)
    new_new = jnp.sum(sides(z) * image)
    old_new = jnp.sum(sides(z_old[...]) * image)
    new_old = jnp.sum(sides(z) * c_old[...])
    line = tag(
        jnp.zeros((1, 128), F32), (0, gamma_new), (1, new_new), (2, old_new), (3, new_old)
    )
    window = jnp.concatenate([line, jnp.zeros((7, 128), F32)], axis=0)
    send[...] = jnp.broadcast_to(window[None], (DEV, 8, 128))
    post(place, live, image, send)


def second(place, live, *rest):
    small = jax.ShapeDtypeStruct((8, NF), F32)
    return pl.pallas_call(
        second_kernel,
        in_specs=[smem(), smem()] + [vmem()] * 10,
        out_shape=[small, small, small, small, jax.ShapeDtypeStruct((DEV, 8, 128), F32)],
        compiler_params=pltpu.CompilerParams(vmem_limit_bytes=40 * 2**20),
        cost_estimate=pl.CostEstimate(flops=10**7, transcendentals=0, bytes_accessed=12 * 2**20),
        name="second",
    )(place, live, *rest)


def last_kernel(place, live, z_old, w_old, z_new, c_new, resid, sums, got, x_out, r_out):
    line = got[0, 0:1, :]
    for e in range(1, DEV):
        line = line + got[e, 0:1, :]
    gamma = pick_lane(sums[0:1, :], 120)
    delta = pick_lane(sums[0:1, :], 121)
    alpha = gamma / delta
    gamma_new = pick_lane(line, 0)
    beta = gamma_new / gamma
    curve = pick_lane(line, 1) + beta * (pick_lane(line, 2) + pick_lane(line, 3)) + beta * beta * delta
    alpha_new = gamma_new / curve
    w = meet(place, live, c_new[...], got)
    search = z_new[...] + beta * z_old[...]
    along = w + beta * w_old[...]
    x = sides(alpha * z_old[...] + alpha_new * search)
    r = sides(resid[...] - alpha_new * along)
    for s in range(2):
        x_out[s, 0] = x[4 * s : 4 * s + 4]
        r_out[s, 0] = r[4 * s : 4 * s + 4]


def last(place, live, *rest):
    out = jax.ShapeDtypeStruct((2, 1, 4, NF), F32)
    return pl.pallas_call(
        last_kernel,
        in_specs=[smem(), smem()] + [vmem()] * 7,
        out_shape=[out, out],
        cost_estimate=pl.CostEstimate(flops=10**6, transcendentals=0, bytes_accessed=2**20),
        name="last",
    )(place, live, *rest)


def shift(value, axis, steps):
    count = lax.axis_size(axis)
    first_, last_ = max(0, -steps), min(count, count - steps)
    return lax.ppermute(value, axis, [(source, source + steps) for source in range(first_, last_)])


def exchange(packet):
    return lax.all_to_all(packet, GX_GY, 0, 0, tiled=True)


def vertex_table(corners, ix, iy):
    number = corners.astype(F32) + 1.0
    upper = number[:, :12].reshape(2, 2, 6)
    lower = number[1:, 12:].reshape(1, 2, 6)
    rows = jnp.concatenate([upper, lower], axis=0)
    keep = jnp.stack([jnp.bool_(True), jnp.bool_(True), ix == GRID_X - 1])
    rows = jnp.where(keep[:, None, None], rows, 0.0)
    line = jnp.transpose(rows, (1, 0, 2)).reshape(2, 18)
    line = jnp.where(jnp.stack([jnp.bool_(True), iy == GRID_Y - 1])[:, None], line, 0.0)
    return lax.dynamic_update_slice(jnp.zeros((2, 128), F32), line, (0, 12 * ix))


def shards(inverse, couple, stiff, basis, loads, order, corner_index, coarse_inverse):
    ix = lax.axis_index(GX)
    iy = lax.axis_index(GY)
    corners = corner_index.reshape(2, NCOR)
    place = jnp.stack([ix, iy]).astype(jnp.int32)
    live = jnp.stack([ix > 0, ix < GRID_X - 1, iy > 0, iy < GRID_Y - 1]).astype(F32)
    table = exchange(jnp.broadcast_to(vertex_table(corners, ix, iy)[None], (DEV, 2, 128)))
    index = jnp.pad(corners.astype(F32), ((0, 0), (0, NF - NCOR))).reshape(2, 1, NF)
    s_full, p_in, p_n, p_s, p_w, p_e = schur(order, inverse, couple, stiff, basis, loads, index)
    q_s = shift(p_n, GX, -1)
    q_n = shift(p_s, GX, 1)
    q_e = shift(p_w, GY, -1)
    q_w = shift(p_e, GY, 1)
    columns = jnp.pad(jnp.transpose(coarse_inverse), ((0, 2), (0, 0)))
    coarse = vertex_order(table, columns)
    finv, tmap, resid, smooth, slots, send = faces(place, live, p_in, p_n, p_s, p_w, p_e, q_n, q_s, q_w, q_e)
    values, _ = owners(exchange(send), coarse)
    z0, c0, send = first(place, live, s_full, tmap, resid, smooth, slots, exchange(values))
    got = exchange(send)
    values, sums = owners(got, coarse)
    z1, c1, w0, r1, send = second(
        place, live, s_full, finv, tmap, resid, z0, c0, slots, exchange(values), sums, got
    )
    got = exchange(send)
    return tuple(last(place, live, z0, w0, z1, c1, r1, sums, got))


def solution(mesh):
    torus = Mesh(mesh.devices.reshape(4, 2, 4, 2, 2), GX_GY)
    in_specs = (
        P(GX, GY, None, None),
        P(GX, GY, None, None),
        P(GX, GY, None, None, None),
        P(GX, GY, None, None),
        P(GX, GY, None, None),
        P(GX, GY, None, None),
        P(GX, GY, None),
        P(None, GX_GY),
    )
    out_specs = (P(GX, GY, None, None), P(GX, GY, None, None))
    return jax.shard_map(shards, mesh=torus, in_specs=in_specs, out_specs=out_specs, check_vma=False)
```

```python
import jax
import jax.numpy as jnp
from jax import lax
from jax.experimental import pallas as pl
from jax.experimental.pallas import tpu as pltpu
from jax.sharding import Mesh
from jax.sharding import PartitionSpec as P

GX = ("gx_0", "gx_1")
GY = ("gy_0", "gy_1", "gy_2")
GX_GY = GX + GY

NI = 1536
NF = 256
NCOR = 24
NCOARSE = 1792
OWN = 14
GRID_X = 8
GRID_Y = 16
DEV = 128
PKT = 288
ONE = 160
TWO = 312
HALF = NF // 2
STEPS = 3
CHUNK = NI // STEPS
VC = 24
F32 = jnp.float32
BF16 = jnp.bfloat16
HIGHEST = lax.Precision.HIGHEST

FACE = ((0, 1, 3, 5), (1, 2, 4, 6))
GROUPS = ((0, 2), (0, 1), (1, 3), (0, 4), (1, 5), (0, 6), (1, 7))
GROUP_ROW = (0, 1, -1, 2, 0, 1, 0, 1)
GROUP_COL = (1, 1, 1, 1, 0, 0, 2, 2)


def nn(a, b):
    return lax.dot_general(a, b, (((1,), (0,)), ((), ())), preferred_element_type=F32)


def nt(a, b):
    return lax.dot_general(a, b, (((1,), (1,)), ((), ())), preferred_element_type=F32)


def split2(x):
    hi = x.astype(BF16)
    return hi, (x - hi.astype(F32)).astype(BF16)


def split3(x):
    hi = x.astype(BF16)
    rest = x - hi.astype(F32)
    mid = rest.astype(BF16)
    return hi, mid, (rest - mid.astype(F32)).astype(BF16)


def iota(shape, dim):
    return lax.broadcasted_iota(jnp.int32, shape, dim)


BLOCK = {}
for f_ in range(4):
    for g_ in range(f_, 4):
        BLOCK[f_, g_] = len(BLOCK)


def schur_kernel(order, inverse, couple, stiff, basis, loads, index, s_out, p_in, p_n, p_s, p_w, p_e, t_n, t_s, t_w, t_e, ct, prod, pick):
    sub = pl.program_id(0)
    step = pl.program_id(1)

    @pl.when(step == 0)
    def _():
        for f in range(4):
            chosen = (iota((NF, NF), 0) == order[f : f + 1, :]).astype(BF16)
            pick[f] = chosen
            ct[f * NF : (f + 1) * NF, :] = nt(chosen, couple[:, f * NF : (f + 1) * NF]).astype(BF16)

    prod[pl.ds(step * CHUNK, CHUNK), :] = nt(inverse[...], ct[...]).astype(BF16)

    @pl.when(step == STEPS - 1)
    def _():
        for f in range(4):
            rows = slice(f * NF, (f + 1) * NF)
            back = nn(ct[rows, :], prod[:, f * NF :])
            chosen = pick[f]
            canon = nt(nn(chosen, stiff[f]).astype(BF16), chosen)
            diag = canon - back[:, :NF]
            s_out[BLOCK[f, f]] = diag.astype(BF16)
            for g in range(f + 1, 4):
                s_out[BLOCK[f, g]] = (-back[:, (g - f) * NF : (g - f + 1) * NF]).astype(BF16)
            lowered = nt(basis[:, f * NF : (f + 1) * NF], chosen).astype(BF16)
            hi, lo = split2(diag)
            corner = nn(lowered, hi) + nn(lowered, lo)
            parts = jnp.concatenate(
                [part.astype(F32) for part in split3(jnp.broadcast_to(loads[f : f + 1, :], (8, NF)))], axis=0
            ).astype(BF16)
            placed = nt(parts, chosen)
            load = placed[0:8] + placed[8:16] + placed[16:24]

            def put(out, lead):
                out[lead + (slice(0, NF), slice(None))] = diag
                out[lead + (slice(NF, NF + NCOR), slice(None))] = corner
                out[lead + (slice(NF + NCOR, NF + NCOR + 8), slice(None))] = jnp.where(iota((8, NF), 0) == 0, load, 0.0)
                out[lead + (slice(NF + NCOR + 1, NF + NCOR + 2), slice(0, NCOR))] = index[...].astype(F32)

            def put_one(out):
                row, col = iota((HALF, HALF), 0), iota((HALF, HALF), 1)
                first_ = diag[:HALF, :HALF]
                out[0:HALF, 0:HALF] = jnp.where(row > col, first_, diag[HALF:, HALF:])
                out[0:HALF, HALF:] = diag[HALF:, :HALF]
                out[HALF : HALF + NCOR, :] = corner
                at = HALF + NCOR
                out[at : at + 8, :] = jnp.where(iota((8, NF), 0) == 0, load, 0.0)
                out[at + 1 : at + 2, 0:NCOR] = index[...].astype(F32)
                out[at + 2 : at + 3, 0:HALF] = jnp.sum(jnp.where(row == col, first_, 0.0), axis=0, keepdims=True)

            def put_two(out, kept):
                row, col = iota((NF, NF), 0), iota((NF, NF), 1)
                first_ = kept[0, 0:NF, :]
                out[0:NF, :] = jnp.where(row > col, first_, diag)
                out[NF : NF + NCOR, :] = kept[0, NF : NF + NCOR, :]
                out[NF + NCOR : NF + 2 * NCOR, :] = corner
                at = NF + 2 * NCOR
                out[at : at + 8, :] = jnp.where(iota((8, NF), 0) == 2, load, 0.0)
                out[at : at + 2, :] = kept[0, NF + NCOR : NF + NCOR + 2, :]
                out[at + 3 : at + 4, 0:NCOR] = index[...].astype(F32)
                out[at + 4 : at + 5, :] = jnp.sum(jnp.where(row == col, first_, 0.0), axis=0, keepdims=True)

            def both(*steps):
                def run():
                    for one in steps:
                        one()

                return run

            if f == 0:
                pl.when(sub == 0)(both(lambda: put(p_n, ()), lambda: put_one(t_n)))
                pl.when(sub == 1)(lambda: put(p_in, (1,)))
            elif f == 1:
                pl.when(sub == 0)(lambda: put(p_in, (0,)))
                pl.when(sub == 1)(both(lambda: put(p_s, ()), lambda: put_one(t_s)))
            else:
                kept, out_ = (p_w, t_w) if f == 2 else (p_e, t_e)
                pl.when(sub == 0)(lambda: put(kept, (0,)))
                pl.when(sub == 1)(both(lambda: put(kept, (1,)), lambda: put_two(out_, kept)))


def schur(order, inverse, couple, stiff, basis, loads, index):
    pkt = pltpu.HBM((PKT, NF), F32)
    pair = pltpu.HBM((2, PKT, NF), F32)
    one = jax.ShapeDtypeStruct((ONE, NF), F32)
    two = jax.ShapeDtypeStruct((TWO, NF), F32)
    return pl.pallas_call(
        schur_kernel,
        grid=(2, STEPS),
        in_specs=[
            pl.BlockSpec((None, None, 4, NF), lambda s, j: (s, 0, 0, 0)),
            pl.BlockSpec((None, None, CHUNK, NI), lambda s, j: (s, 0, j, 0)),
            pl.BlockSpec((None, None, NI, 4 * NF), lambda s, j: (s, 0, 0, 0)),
            pl.BlockSpec((None, None, 4, NF, NF), lambda s, j: (s, 0, 0, 0, 0)),
            pl.BlockSpec((None, None, NCOR, 4 * NF), lambda s, j: (s, 0, 0, 0)),
            pl.BlockSpec((None, None, 4, NF), lambda s, j: (s, 0, 0, 0)),
            pl.BlockSpec((None, 1, NCOR), lambda s, j: (s, 0, 0)),
        ],
        out_specs=[
            pl.BlockSpec((None, 10, NF, NF), lambda s, j: (s, 0, 0, 0)),
            pl.BlockSpec((2, PKT, NF), lambda s, j: (0, 0, 0)),
            pl.BlockSpec((PKT, NF), lambda s, j: (0, 0)),
            pl.BlockSpec((PKT, NF), lambda s, j: (0, 0)),
            pl.BlockSpec((2, PKT, NF), lambda s, j: (0, 0, 0)),
            pl.BlockSpec((2, PKT, NF), lambda s, j: (0, 0, 0)),
            pl.BlockSpec((ONE, NF), lambda s, j: (0, 0)),
            pl.BlockSpec((ONE, NF), lambda s, j: (0, 0)),
            pl.BlockSpec((TWO, NF), lambda s, j: (0, 0)),
            pl.BlockSpec((TWO, NF), lambda s, j: (0, 0)),
        ],
        out_shape=[jax.ShapeDtypeStruct((2, 10, NF, NF), BF16), pair, pkt, pkt, pair, pair, one, one, two, two],
        scratch_shapes=[
            pltpu.VMEM((4 * NF, NI), BF16),
            pltpu.VMEM((NI, 4 * NF), BF16),
            pltpu.VMEM((4, NF, NF), BF16),
        ],
        compiler_params=pltpu.CompilerParams(
            dimension_semantics=("arbitrary", "arbitrary"), vmem_limit_bytes=40 * 2**20
        ),
        cost_estimate=pl.CostEstimate(flops=16 * 10**9, transcendentals=0, bytes_accessed=32 * 2**20),
        name="schur",
    )(*(pltpu.with_memory_space_constraint(x, pltpu.HBM) for x in (order, inverse, couple, stiff, basis, loads, index)))


def spread_window(place, contributions):
    corner = iota((NCOR, 128), 0)
    lane = iota((NCOR, 128), 1)
    below = jnp.where(corner >= 12, 1, 0)
    inside = corner - 12 * below
    right = inside >= 6
    dof = inside - jnp.where(right, 6, 0)
    cols = [jnp.zeros((1, 128), F32) for _ in range(4)]
    for g, value in contributions.items():
        target = (2 * place[0] + GROUP_ROW[g] + below) * 6 + dof
        filled = jnp.where(lane == target, jnp.broadcast_to(value, (NCOR, 128)), 0.0)
        left = jnp.sum(jnp.where(right, 0.0, filled), axis=0, keepdims=True)
        both = jnp.sum(filled, axis=0, keepdims=True)
        cols[GROUP_COL[g]] = cols[GROUP_COL[g]] + left
        cols[GROUP_COL[g] + 1] = cols[GROUP_COL[g] + 1] + (both - left)
    return cols


def row_dot(matrix, row):
    return jnp.sum(matrix * row, axis=1, keepdims=True)


def face_kernel(
    place, live, h_in, h_n, h_s, h_w, h_e, q_n, q_s, q_w, q_e, finv, tmap, r_out, z_out, slots, send,
    a_hi, a_lo, x, p_in, p_n, p_s, p_w, p_e, sems
):
    sources = (h_in, h_n, h_s, h_w, h_e)
    targets = (p_in, p_n, p_s, p_w, p_e)
    copies = [pltpu.make_async_copy(sources[i], targets[i], sems.at[i]) for i in range(5)]
    for copy in copies:
        copy.start()
    for copy in copies:
        copy.wait()

    def kept(m):
        return (p_n, p_in.at[0], p_s, p_w.at[0], p_w.at[1], p_e.at[0], p_e.at[1])[m]

    def alive(m):
        return (live[0], 1.0, live[1], live[2], live[2], live[3], live[3])[m]

    def own_part(m, start_, count):
        return kept(m)[start_ : start_ + count, :]

    def other_part(m, start_, count):
        if m == 1:
            return p_in[1, NF + start_ : NF + start_ + count, :]
        if m in (0, 2):
            at = HALF + start_
            return (q_n if m == 0 else q_s)[at : at + count, :]
        side = q_w if m < 5 else q_e
        which = (m - 3) % 2
        at = NF + NCOR * which if start_ == 0 else NF + 2 * NCOR + 2 * which + start_ - NCOR
        return side[at : at + count, :]

    def one_square(q):
        row, col = iota((HALF, HALF), 0), iota((HALF, HALF), 1)
        square = q[0:HALF, 0:HALF]
        low = q[0:HALF, HALF:]
        turned = jnp.transpose(square)
        line = q[HALF + NCOR + 2 : HALF + NCOR + 3, 0:HALF]
        upper = jnp.where(row > col, square, jnp.where(row < col, turned, line))
        lower = jnp.where(row > col, turned, square)
        return jnp.concatenate(
            [jnp.concatenate([upper, jnp.transpose(low)], axis=1), jnp.concatenate([low, lower], axis=1)], axis=0
        )

    def two_squares(q):
        row, col = iota((NF, NF), 0), iota((NF, NF), 1)
        square = q[0:NF, :]
        turned = jnp.transpose(square)
        line = q[NF + 2 * NCOR + 4 : NF + 2 * NCOR + 5, :]
        return (
            jnp.where(row > col, square, jnp.where(row < col, turned, line)),
            jnp.where(row > col, turned, square),
        )

    others = (one_square(q_n), p_in[1, 0:NF, :], one_square(q_s), *two_squares(q_w), *two_squares(q_e))
    eye = jnp.where(iota((NF, NF), 0) == iota((NF, NF), 1), 1.0, 0.0)
    guess = []
    for m in range(7):
        full = own_part(m, 0, NF) + others[m]
        hi, lo = split2(full)
        a_hi[m] = hi
        a_lo[m] = lo
        size = jnp.max(jnp.sum(jnp.abs(full), axis=0, keepdims=True))
        scale = 1.9 / size
        guess.append(scale)
        x[m] = scale * (2.0 * eye - scale * full)

    def rough(state):
        count, _ = state
        worst = jnp.float32(0.0)
        for m in range(7):
            now = x[m]
            near = now.astype(BF16)
            left = eye - nn(a_hi[m], near)
            worst = jnp.maximum(worst, jnp.sum(left * left))
            x[m] = now + nn(near, left.astype(BF16))
        return count + 1, worst

    def rough_on(state):
        count, worst = state
        return jnp.logical_and(count < 24, jnp.logical_not(worst < 0.1))

    _, worst = lax.while_loop(rough_on, rough, (jnp.int32(0), jnp.float32(1e9)))
    fine_start = worst < 0.1

    @pl.when(jnp.logical_not(fine_start))
    def _():
        for m in range(7):
            x[m] = guess[m] * eye

    def fine(state):
        count, _ = state
        worst = jnp.float32(0.0)
        for m in range(7):
            now = x[m]
            hi, lo = split2(now)
            left = eye - (nn(a_hi[m], hi) + (nn(a_hi[m], lo) + nn(a_lo[m], hi)))
            worst = jnp.maximum(worst, jnp.sum(left * left))
            x[m] = now + nn(hi, left.astype(BF16))
        return count + 1, worst

    def fine_on(state):
        count, worst = state
        return jnp.logical_and(count < 60, jnp.logical_not(worst < 1e-3))

    lax.while_loop(fine_on, fine, (jnp.int32(0), jnp.float32(1e9)))

    gathered = {}

    def gather(g, value):
        gathered[g] = value if g not in gathered else gathered[g] + value

    rows_r = []
    rows_i = [None] * 8
    for m in range(7):
        inverse = x[m] * alive(m)
        finv[m] = inverse
        both = jnp.concatenate([own_part(m, NF, NCOR), other_part(m, 0, NCOR)], axis=0)
        b_hi, b_lo = split2(both)
        i_hi, i_lo = split2(inverse)
        lifted = nn(jnp.concatenate([b_hi, b_lo], axis=0), i_hi)
        mapped = lifted[:48] + lifted[48:] + nn(b_hi, i_lo)
        tmap[m] = mapped
        resid = alive(m) * (own_part(m, NF + NCOR, 1) + other_part(m, NCOR, 1))
        rows_r.append(resid)
        gather(GROUPS[m][0], row_dot(mapped[:NCOR], resid))
        if m == 1:
            gather(GROUPS[m][1], row_dot(mapped[NCOR:], resid))
        rows_i[GROUPS[m][0]] = own_part(m, NF + NCOR + 1, 1)[:, 0:128]
        rows_i[GROUPS[m][1]] = other_part(m, NCOR + 1, 1)[:, 0:128]
    resid = jnp.concatenate(rows_r + [jnp.zeros((1, NF), F32)], axis=0)
    r_out[...] = resid
    z_out[...] = face_apply(finv, resid)
    numbers = jnp.transpose(jnp.concatenate(rows_i, axis=0))[:NCOR, :]
    slots[...] = numbers
    sums = spread_window(place, gathered)
    upper = iota((NCOR, 1), 0) < 12
    named = {0: jnp.where(upper, numbers[:, 0:1] + 1.0, 0.0)}
    keep = jnp.logical_or(upper, place[0] == GRID_X - 1)
    named[1] = jnp.where(keep, numbers[:, 1:2] + 1.0, 0.0)
    names = spread_window(place, named)
    edge = jnp.where(place[1] == GRID_Y - 1, names[2], 0.0)
    send[...] = jnp.broadcast_to(jnp.concatenate([sums[1], sums[2], names[1], edge], axis=1), (DEV, 512))


def face_apply(finv, rows):
    turned = jnp.transpose(rows)
    outs = [jnp.sum(finv[m] * turned[:, m : m + 1], axis=0, keepdims=True) for m in range(7)]
    return jnp.concatenate(outs + [jnp.zeros((1, NF), F32)], axis=0)


def smem():
    return pl.BlockSpec(memory_space=pltpu.SMEM)


def vmem():
    return pl.BlockSpec(memory_space=pltpu.VMEM)


def faces(place, live, *packets):
    return pl.pallas_call(
        face_kernel,
        in_specs=[smem(), smem()] + [pl.BlockSpec(memory_space=pl.ANY)] * 5 + [vmem()] * 4,
        out_shape=[
            jax.ShapeDtypeStruct((7, NF, NF), F32),
            jax.ShapeDtypeStruct((7, 48, NF), F32),
            jax.ShapeDtypeStruct((8, NF), F32),
            jax.ShapeDtypeStruct((8, NF), F32),
            jax.ShapeDtypeStruct((NCOR, 8), F32),
            jax.ShapeDtypeStruct((DEV, 512), F32),
        ],
        scratch_shapes=[
            pltpu.VMEM((7, NF, NF), BF16),
            pltpu.VMEM((7, NF, NF), BF16),
            pltpu.VMEM((7, NF, NF), F32),
            pltpu.VMEM((2, PKT, NF), F32),
            pltpu.VMEM((PKT, NF), F32),
            pltpu.VMEM((PKT, NF), F32),
            pltpu.VMEM((2, PKT, NF), F32),
            pltpu.VMEM((2, PKT, NF), F32),
            pltpu.SemaphoreType.DMA((5,)),
        ],
        compiler_params=pltpu.CompilerParams(vmem_limit_bytes=16 * 2**20),
        cost_estimate=pl.CostEstimate(flops=5 * 10**9, transcendentals=0, bytes_accessed=10 * 2**20),
        name="faces",
    )(place, live, *packets)


def total_rows(got):
    total = got[0:GRID_Y, 0:512]
    for ix in range(1, GRID_X):
        total = total + got[ix * GRID_Y : (ix + 1) * GRID_Y, 0:512]
    return total


def owner_line(inverse, grid):
    partial = jnp.zeros((16, 128), F32)
    for col in range(1, 18):
        partial = partial + inverse[col] * grid[col : col + 1, :]
    column = jnp.sum(partial, axis=1, keepdims=True)
    return jnp.sum(jnp.where(iota((16, 128), 0) == iota((16, 128), 1), column, 0.0), axis=0, keepdims=True)


def start_kernel(got, columns, inverse, out, grid, table, padded):
    total = total_rows(got)
    grid[...] = jnp.zeros((VC, 128), F32)
    grid[1:17, :] = total[:, 0:128]
    grid[2:18, :] = grid[2:18, :] + total[:, 128:256]
    table[1:17, :] = total[:, 256:384]
    table[17:18, :] = total[GRID_Y - 1 : GRID_Y, 384:512]
    padded[...] = jnp.zeros((16, NCOARSE), F32)
    padded[0:OWN, :] = columns[...]
    lhs = jnp.concatenate(split3(padded[...]), axis=0)
    rows = iota((NCOARSE, 256), 0) + 1
    for pair in range(9):
        first_ = table[2 * pair + 1 : 2 * pair + 2, :]
        second_ = table[2 * pair + 2 : 2 * pair + 3, :] if pair < 8 else jnp.zeros((1, 128), F32)
        wanted = jnp.concatenate([first_, second_], axis=1).astype(jnp.int32)
        got_ = nn(lhs, (rows == wanted).astype(BF16))
        got_ = got_[0:16] + got_[16:32] + got_[32:48]
        inverse[2 * pair + 1] = got_[:, :128]
        if pair < 8:
            inverse[2 * pair + 2] = got_[:, 128:]
    for other in (0, *range(18, VC)):
        inverse[other] = jnp.zeros((16, 128), F32)
    out[...] = jnp.broadcast_to(owner_line(inverse, grid), (DEV, 128))


def start(got, columns):
    return pl.pallas_call(
        start_kernel,
        out_shape=[jax.ShapeDtypeStruct((VC, 16, 128), F32), jax.ShapeDtypeStruct((DEV, 128), F32)],
        scratch_shapes=[pltpu.VMEM((VC, 128), F32), pltpu.VMEM((VC, 128), F32), pltpu.VMEM((16, NCOARSE), F32)],
        compiler_params=pltpu.CompilerParams(vmem_limit_bytes=8 * 2**20),
        cost_estimate=pl.CostEstimate(flops=10**9, transcendentals=0, bytes_accessed=2**20),
        name="start",
    )(got, columns)


def owner_kernel(place, live, got, inverse, image, out, sums, grid):
    total = total_rows(got)
    grid[...] = jnp.zeros((VC, 128), F32)
    for vc in range(4):
        grid[vc : vc + GRID_Y, :] = grid[vc : vc + GRID_Y, :] + total[:, vc * 128 : (vc + 1) * 128]
    sums[...] = jnp.broadcast_to(jnp.sum(total[:, 0:128], axis=0, keepdims=True), (8, 128))
    out[:, 0:128] = jnp.broadcast_to(owner_line(inverse, grid), (DEV, 128))
    out[:, 128:] = jnp.zeros((DEV, 512), F32)
    post(place, live, image, out)


def owners(place, live, got, inverse, image):
    return pl.pallas_call(
        owner_kernel,
        in_specs=[smem(), smem()] + [vmem()] * 3,
        out_shape=[jax.ShapeDtypeStruct((DEV, 640), F32), jax.ShapeDtypeStruct((8, 128), F32)],
        scratch_shapes=[pltpu.VMEM((VC, 128), F32)],
        compiler_params=pltpu.CompilerParams(vmem_limit_bytes=6 * 2**20),
        cost_estimate=pl.CostEstimate(flops=10**6, transcendentals=0, bytes_accessed=2**20),
        name="owners",
    )(place, live, got, inverse, image)


def coarse_values(slots, coarse):
    lane = iota((NCOR, 128), 1).astype(F32)
    owner_rows = []
    places = []
    for g in range(8):
        number = slots[:, g : g + 1]
        owner = jnp.floor((number + 0.5) * (1.0 / OWN))
        places.append(number - OWN * owner)
        owner_rows.append(jnp.where(lane == owner, 1.0, 0.0))
    picked = lax.dot_general(
        jnp.concatenate(owner_rows, axis=0),
        coarse[:, 0:128],
        (((1,), (0,)), ((), ())),
        precision=HIGHEST,
        preferred_element_type=F32,
    )
    return [
        jnp.sum(jnp.where(lane == places[g], picked[g * NCOR : (g + 1) * NCOR], 0.0), axis=1, keepdims=True)
        for g in range(8)
    ]


def prolong(tmap, values):
    outs = []
    for m in range(7):
        column = jnp.concatenate([values[GROUPS[m][0]], values[GROUPS[m][1]]], axis=0)
        outs.append(jnp.sum(tmap[m] * column, axis=0, keepdims=True))
    return jnp.concatenate(outs + [jnp.zeros((1, NF), F32)], axis=0)


def subdomain_apply(s_ref, vector):
    turned = jnp.transpose(vector)
    rows = []
    for s in range(2):
        across = [None] * 4
        upright = [None] * 4
        for f in range(4):
            column = turned[:, FACE[s][f] : FACE[s][f] + 1]
            for g in range(f, 4):
                block = s_ref[s, BLOCK[f, g]].astype(F32)
                down = jnp.sum(block * column, axis=0, keepdims=True)
                across[g] = down if across[g] is None else across[g] + down
                if g > f:
                    m = FACE[s][g]
                    side = row_dot(block, vector[m : m + 1, :])
                    upright[f] = side if upright[f] is None else upright[f] + side
        columns = jnp.concatenate(
            [jnp.broadcast_to(upright[f], (NF, 128)) if f < 3 else jnp.zeros((NF, 128), F32) for f in range(4)], axis=1
        )
        lane_pick = jnp.concatenate([columns[:, f * 128 : f * 128 + 1] for f in range(4)] * 2, axis=1)
        flipped = jnp.transpose(lane_pick)
        for f in range(4):
            rows.append(across[f] + flipped[f : f + 1, :])
    return jnp.concatenate(rows, axis=0)


def restrict(place, tmap, image):
    gathered = {}

    def gather(g, value):
        gathered[g] = value if g not in gathered else gathered[g] + value

    for m in range(7):
        line = None
        for s in range(2):
            for f in range(4):
                if FACE[s][f] == m:
                    row = image[s * 4 + f : s * 4 + f + 1, :]
                    line = row if line is None else line + row
        gather(GROUPS[m][0], row_dot(tmap[m, 0:NCOR], line))
        gather(GROUPS[m][1], row_dot(tmap[m, NCOR:], line))
    return spread_window(place, gathered)


def post(place, live, image, send):
    me = place[0] * GRID_Y + place[1]

    def put(target, slot, row):
        at = pl.ds(target, 1)
        send[at, slot * 128 : slot * 128 + NF] = image[row : row + 1, :]

    @pl.when(live[0] > 0.0)
    def _():
        put(me - GRID_Y, 1, 0)

    @pl.when(live[1] > 0.0)
    def _():
        put(me + GRID_Y, 1, 5)

    @pl.when(live[2] > 0.0)
    def _():
        put(me - 1, 1, 2)
        put(me - 1, 3, 6)

    @pl.when(live[3] > 0.0)
    def _():
        put(me + 1, 1, 3)
        put(me + 1, 3, 7)


def meet(place, live, image, got):
    me = place[0] * GRID_Y + place[1]

    def read(source, slot, alive):
        at = jnp.clip(source, 0, DEV - 1)
        row = got[pl.ds(at, 1), slot * 128 : slot * 128 + NF]
        return jnp.where(alive > 0.0, row, 0.0)

    def mine(row):
        return image[row : row + 1, :]

    return jnp.concatenate(
        [
            live[0] * (mine(0) + read(me - GRID_Y, 1, live[0])),
            mine(1) + mine(4),
            live[1] * (mine(5) + read(me + GRID_Y, 1, live[1])),
            live[2] * (mine(2) + read(me - 1, 1, live[2])),
            live[2] * (mine(6) + read(me - 1, 3, live[2])),
            live[3] * (mine(3) + read(me + 1, 1, live[3])),
            live[3] * (mine(7) + read(me + 1, 3, live[3])),
            jnp.zeros((1, NF), F32),
        ],
        axis=0,
    )


def shared_dot(first, second):
    weight = jnp.where(iota((8, NF), 0) == 1, 1.0, 0.5)
    return jnp.sum(weight * first * second)


def sides(vector):
    return jnp.concatenate([vector[m : m + 1, :] for s in range(2) for m in FACE[s]], axis=0)


def tag(row, *scalars):
    lane = iota((1, 128), 1)
    for at, value in scalars:
        row = jnp.where(lane == at, value, row)
    return row


def first_kernel(place, live, s_ref, tmap, resid, smooth, slots, coarse, z_out, c_out, send):
    z = smooth[...] + prolong(tmap, coarse_values(slots, coarse))
    z_out[...] = z
    image = subdomain_apply(s_ref, z)
    c_out[...] = image
    cols = restrict(place, tmap, image)
    gamma = shared_dot(resid[...], z)
    delta = jnp.sum(sides(z) * image)
    cols[0] = tag(cols[0], (120, gamma), (121, delta))
    send[...] = jnp.broadcast_to(jnp.concatenate(cols, axis=1), (DEV, 512))


def first(place, live, *rest):
    return pl.pallas_call(
        first_kernel,
        in_specs=[smem(), smem()] + [vmem()] * 6,
        out_shape=[
            jax.ShapeDtypeStruct((8, NF), F32),
            jax.ShapeDtypeStruct((8, NF), F32),
            jax.ShapeDtypeStruct((DEV, 512), F32),
        ],
        compiler_params=pltpu.CompilerParams(vmem_limit_bytes=10 * 2**20),
        cost_estimate=pl.CostEstimate(flops=10**7, transcendentals=0, bytes_accessed=10 * 2**20),
        name="first",
    )(place, live, *rest)


def pick_lane(row, at):
    return jnp.sum(jnp.where(iota((1, 128), 1) == at, row, 0.0))


def second_kernel(place, live, s_ref, finv, tmap, resid, z_old, c_old, slots, sums, got, z_out, c_out, w_out, r_out, send):
    gamma = pick_lane(sums[0:1, :], 120)
    delta = pick_lane(sums[0:1, :], 121)
    alpha = gamma / delta
    w = meet(place, live, c_old, got)
    w_out[...] = w
    y = face_apply(finv, w) + prolong(tmap, coarse_values(slots, got))
    z = z_old[...] - alpha * y
    r = resid[...] - alpha * w
    z_out[...] = z
    r_out[...] = r
    image = subdomain_apply(s_ref, z)
    c_out[...] = image
    gamma_new = shared_dot(r, z)
    new_new = jnp.sum(sides(z) * image)
    old_new = jnp.sum(sides(z_old[...]) * image)
    new_old = jnp.sum(sides(z) * c_old[...])
    line = tag(
        jnp.zeros((1, 128), F32), (0, gamma_new), (1, new_new), (2, old_new), (3, new_old)
    )
    send[:, 0:128] = jnp.broadcast_to(line, (DEV, 128))
    send[:, 128:] = jnp.zeros((DEV, 512), F32)
    post(place, live, image, send)


def second(place, live, *rest):
    small = jax.ShapeDtypeStruct((8, NF), F32)
    return pl.pallas_call(
        second_kernel,
        in_specs=[smem(), smem()] + [vmem()] * 9,
        out_shape=[small, small, small, small, jax.ShapeDtypeStruct((DEV, 640), F32)],
        compiler_params=pltpu.CompilerParams(vmem_limit_bytes=14 * 2**20),
        cost_estimate=pl.CostEstimate(flops=10**7, transcendentals=0, bytes_accessed=12 * 2**20),
        name="second",
    )(place, live, *rest)


def last_kernel(place, live, z_old, w_old, z_new, c_new, resid, sums, got, x_out, r_out):
    line = jnp.sum(got[:, 0:128], axis=0, keepdims=True)
    gamma = pick_lane(sums[0:1, :], 120)
    delta = pick_lane(sums[0:1, :], 121)
    alpha = gamma / delta
    gamma_new = pick_lane(line, 0)
    beta = gamma_new / gamma
    curve = pick_lane(line, 1) + beta * (pick_lane(line, 2) + pick_lane(line, 3)) + beta * beta * delta
    alpha_new = gamma_new / curve
    w = meet(place, live, c_new[...], got)
    search = z_new[...] + beta * z_old[...]
    along = w + beta * w_old[...]
    x = sides(alpha * z_old[...] + alpha_new * search)
    r = sides(resid[...] - alpha_new * along)
    for s in range(2):
        x_out[s, 0] = x[4 * s : 4 * s + 4]
        r_out[s, 0] = r[4 * s : 4 * s + 4]


def last(place, live, *rest):
    out = jax.ShapeDtypeStruct((2, 1, 4, NF), F32)
    return pl.pallas_call(
        last_kernel,
        in_specs=[smem(), smem()] + [vmem()] * 7,
        out_shape=[out, out],
        compiler_params=pltpu.CompilerParams(vmem_limit_bytes=6 * 2**20),
        cost_estimate=pl.CostEstimate(flops=10**6, transcendentals=0, bytes_accessed=2**20),
        name="last",
    )(place, live, *rest)


def shift(value, axis, steps):
    count = lax.axis_size(axis)
    first_, last_ = max(0, -steps), min(count, count - steps)
    return lax.ppermute(value, axis, [(source, source + steps) for source in range(first_, last_)])


def exchange(packet):
    return lax.all_to_all(packet, GX_GY, 0, 0, tiled=True)


def shards(inverse, couple, stiff, basis, loads, order, corner_index, coarse_inverse):
    ix = lax.axis_index(GX)
    iy = lax.axis_index(GY)
    place = jnp.stack([ix, iy]).astype(jnp.int32)
    live = jnp.stack([ix > 0, ix < GRID_X - 1, iy > 0, iy < GRID_Y - 1]).astype(F32)
    s_full, p_in, p_n, p_s, p_w, p_e, t_n, t_s, t_w, t_e = schur(order, inverse, couple, stiff, basis, loads, corner_index)
    q_s = shift(t_n, GX, -1)
    q_n = shift(t_s, GX, 1)
    q_e = shift(t_w, GY, -1)
    q_w = shift(t_e, GY, 1)
    finv, tmap, resid, smooth, slots, send = faces(
        place, live, *(pltpu.with_memory_space_constraint(p, pltpu.HBM) for p in (p_in, p_n, p_s, p_w, p_e)), q_n, q_s, q_w, q_e
    )
    coarse, values = start(exchange(send), jnp.transpose(coarse_inverse))
    z0, c0, send = first(place, live, s_full, tmap, resid, smooth, slots, exchange(values))
    send, sums = owners(place, live, exchange(send), coarse, c0)
    z1, c1, w0, r1, send = second(place, live, s_full, finv, tmap, resid, z0, c0, slots, sums, exchange(send))
    return tuple(last(place, live, z0, w0, z1, c1, r1, sums, exchange(send)))


def solution(mesh):
    torus = Mesh(mesh.devices.reshape(4, 2, 4, 2, 2), GX_GY)
    in_specs = (
        P(GX, GY, None, None),
        P(GX, GY, None, None),
        P(GX, GY, None, None, None),
        P(GX, GY, None, None),
        P(GX, GY, None, None),
        P(GX, GY, None, None),
        P(GX, GY, None),
        P(None, GX_GY),
    )
    out_specs = (P(GX, GY, None, None), P(GX, GY, None, None))
    return jax.shard_map(shards, mesh=torus, in_specs=in_specs, out_specs=out_specs, check_vma=False)
```

```python
import jax
import jax.numpy as jnp
from jax import lax
from jax.experimental import pallas as pl
from jax.experimental.pallas import tpu as pltpu
from jax.sharding import Mesh
from jax.sharding import PartitionSpec as P

GX = ("gx_0", "gx_1")
GY = ("gy_0", "gy_1", "gy_2")
GX_GY = GX + GY

NI = 1536
NF = 256
NCOR = 24
NCOARSE = 1792
OWN = 14
GRID_X = 8
GRID_Y = 16
DEV = 128
PKT = 288
ONE = 160
TWO = 312
HALF = NF // 2
STEPS = 3
CHUNK = NI // STEPS
VC = 24
F32 = jnp.float32
BF16 = jnp.bfloat16
HIGHEST = lax.Precision.HIGHEST

FACE = ((0, 1, 3, 5), (1, 2, 4, 6))
GROUPS = ((0, 2), (0, 1), (1, 3), (0, 4), (1, 5), (0, 6), (1, 7))
GROUP_ROW = (0, 1, -1, 2, 0, 1, 0, 1)
GROUP_COL = (1, 1, 1, 1, 0, 0, 2, 2)


def nn(a, b):
    return lax.dot_general(a, b, (((1,), (0,)), ((), ())), preferred_element_type=F32)


def nt(a, b):
    return lax.dot_general(a, b, (((1,), (1,)), ((), ())), preferred_element_type=F32)


def split2(x):
    hi = x.astype(BF16)
    return hi, (x - hi.astype(F32)).astype(BF16)


def split3(x):
    hi = x.astype(BF16)
    rest = x - hi.astype(F32)
    mid = rest.astype(BF16)
    return hi, mid, (rest - mid.astype(F32)).astype(BF16)


def iota(shape, dim):
    return lax.broadcasted_iota(jnp.int32, shape, dim)


BLOCK = {}
for f_ in range(4):
    for g_ in range(f_, 4):
        BLOCK[f_, g_] = len(BLOCK)


def schur_kernel(order, inverse, couple, stiff, basis, loads, index, s_out, p_in, p_n, p_s, p_w, p_e, t_n, t_s, t_w, t_e, ct, prod, pick):
    sub = pl.program_id(0)
    step = pl.program_id(1)

    @pl.when(step == 0)
    def _():
        for f in range(4):
            chosen = (iota((NF, NF), 0) == order[f : f + 1, :]).astype(BF16)
            pick[f] = chosen
            ct[f * NF : (f + 1) * NF, :] = nt(chosen, couple[:, f * NF : (f + 1) * NF]).astype(BF16)

    prod[pl.ds(step * CHUNK, CHUNK), :] = nt(inverse[...], ct[...]).astype(BF16)

    @pl.when(step == STEPS - 1)
    def _():
        for f in range(4):
            rows = slice(f * NF, (f + 1) * NF)
            back = nn(ct[rows, :], prod[:, f * NF :])
            chosen = pick[f]
            canon = nt(nn(chosen, stiff[f]).astype(BF16), chosen)
            diag = canon - back[:, :NF]
            s_out[BLOCK[f, f]] = diag.astype(BF16)
            for g in range(f + 1, 4):
                s_out[BLOCK[f, g]] = (-back[:, (g - f) * NF : (g - f + 1) * NF]).astype(BF16)
            lowered = nt(basis[:, f * NF : (f + 1) * NF], chosen).astype(BF16)
            hi, lo = split2(diag)
            corner = nn(lowered, hi) + nn(lowered, lo)
            parts = jnp.concatenate(
                [part.astype(F32) for part in split3(jnp.broadcast_to(loads[f : f + 1, :], (8, NF)))], axis=0
            ).astype(BF16)
            placed = nt(parts, chosen)
            load = placed[0:8] + placed[8:16] + placed[16:24]

            def put(out, lead):
                out[lead + (slice(0, NF), slice(None))] = diag
                out[lead + (slice(NF, NF + NCOR), slice(None))] = corner
                out[lead + (slice(NF + NCOR, NF + NCOR + 8), slice(None))] = jnp.where(iota((8, NF), 0) == 0, load, 0.0)
                out[lead + (slice(NF + NCOR + 1, NF + NCOR + 2), slice(0, NCOR))] = index[...].astype(F32)

            def put_one(out):
                row, col = iota((HALF, HALF), 0), iota((HALF, HALF), 1)
                first_ = diag[:HALF, :HALF]
                out[0:HALF, 0:HALF] = jnp.where(row > col, first_, diag[HALF:, HALF:])
                out[0:HALF, HALF:] = diag[HALF:, :HALF]
                out[HALF : HALF + NCOR, :] = corner
                at = HALF + NCOR
                out[at : at + 8, :] = jnp.where(iota((8, NF), 0) == 0, load, 0.0)
                out[at + 1 : at + 2, 0:NCOR] = index[...].astype(F32)
                out[at + 2 : at + 3, 0:HALF] = jnp.sum(jnp.where(row == col, first_, 0.0), axis=0, keepdims=True)

            def put_two(out, kept):
                row, col = iota((NF, NF), 0), iota((NF, NF), 1)
                first_ = kept[0, 0:NF, :]
                out[0:NF, :] = jnp.where(row > col, first_, diag)
                out[NF : NF + NCOR, :] = kept[0, NF : NF + NCOR, :]
                out[NF + NCOR : NF + 2 * NCOR, :] = corner
                at = NF + 2 * NCOR
                out[at : at + 8, :] = jnp.where(iota((8, NF), 0) == 2, load, 0.0)
                out[at : at + 2, :] = kept[0, NF + NCOR : NF + NCOR + 2, :]
                out[at + 3 : at + 4, 0:NCOR] = index[...].astype(F32)
                out[at + 4 : at + 5, :] = jnp.sum(jnp.where(row == col, first_, 0.0), axis=0, keepdims=True)

            def both(*steps):
                def run():
                    for one in steps:
                        one()

                return run

            if f == 0:
                pl.when(sub == 0)(both(lambda: put(p_n, ()), lambda: put_one(t_n)))
                pl.when(sub == 1)(lambda: put(p_in, (1,)))
            elif f == 1:
                pl.when(sub == 0)(lambda: put(p_in, (0,)))
                pl.when(sub == 1)(both(lambda: put(p_s, ()), lambda: put_one(t_s)))
            else:
                kept, out_ = (p_w, t_w) if f == 2 else (p_e, t_e)
                pl.when(sub == 0)(lambda: put(kept, (0,)))
                pl.when(sub == 1)(both(lambda: put(kept, (1,)), lambda: put_two(out_, kept)))


def schur(order, inverse, couple, stiff, basis, loads, index):
    pkt = pltpu.HBM((PKT, NF), F32)
    pair = pltpu.HBM((2, PKT, NF), F32)
    one = jax.ShapeDtypeStruct((ONE, NF), F32)
    two = jax.ShapeDtypeStruct((TWO, NF), F32)
    return pl.pallas_call(
        schur_kernel,
        grid=(2, STEPS),
        in_specs=[
            pl.BlockSpec((None, None, 4, NF), lambda s, j: (s, 0, 0, 0)),
            pl.BlockSpec((None, None, CHUNK, NI), lambda s, j: (s, 0, j, 0)),
            pl.BlockSpec((None, None, NI, 4 * NF), lambda s, j: (s, 0, 0, 0)),
            pl.BlockSpec((None, None, 4, NF, NF), lambda s, j: (s, 0, 0, 0, 0)),
            pl.BlockSpec((None, None, NCOR, 4 * NF), lambda s, j: (s, 0, 0, 0)),
            pl.BlockSpec((None, None, 4, NF), lambda s, j: (s, 0, 0, 0)),
            pl.BlockSpec((None, 1, NCOR), lambda s, j: (s, 0, 0)),
        ],
        out_specs=[
            pl.BlockSpec((None, 10, NF, NF), lambda s, j: (s, 0, 0, 0)),
            pl.BlockSpec((2, PKT, NF), lambda s, j: (0, 0, 0)),
            pl.BlockSpec((PKT, NF), lambda s, j: (0, 0)),
            pl.BlockSpec((PKT, NF), lambda s, j: (0, 0)),
            pl.BlockSpec((2, PKT, NF), lambda s, j: (0, 0, 0)),
            pl.BlockSpec((2, PKT, NF), lambda s, j: (0, 0, 0)),
            pl.BlockSpec((ONE, NF), lambda s, j: (0, 0)),
            pl.BlockSpec((ONE, NF), lambda s, j: (0, 0)),
            pl.BlockSpec((TWO, NF), lambda s, j: (0, 0)),
            pl.BlockSpec((TWO, NF), lambda s, j: (0, 0)),
        ],
        out_shape=[jax.ShapeDtypeStruct((2, 10, NF, NF), BF16), pair, pkt, pkt, pair, pair, one, one, two, two],
        scratch_shapes=[
            pltpu.VMEM((4 * NF, NI), BF16),
            pltpu.VMEM((NI, 4 * NF), BF16),
            pltpu.VMEM((4, NF, NF), BF16),
        ],
        compiler_params=pltpu.CompilerParams(
            dimension_semantics=("arbitrary", "arbitrary"), vmem_limit_bytes=40 * 2**20
        ),
        cost_estimate=pl.CostEstimate(flops=16 * 10**9, transcendentals=0, bytes_accessed=32 * 2**20),
        name="schur",
    )(*(pltpu.with_memory_space_constraint(x, pltpu.HBM) for x in (order, inverse, couple, stiff, basis, loads, index)))


def spread_window(contributions):
    corner = iota((NCOR, 32), 0)
    lane = iota((NCOR, 32), 1)
    below = jnp.where(corner >= 12, 1, 0)
    inside = corner - 12 * below
    right = inside >= 6
    dof = inside - jnp.where(right, 6, 0)
    cols = [jnp.zeros((1, 32), F32) for _ in range(4)]
    for g, value in contributions.items():
        target = (GROUP_ROW[g] + 1 + below) * 6 + dof
        filled = jnp.where(lane == target, jnp.broadcast_to(value, (NCOR, 32)), 0.0)
        left = jnp.sum(jnp.where(right, 0.0, filled), axis=0, keepdims=True)
        both = jnp.sum(filled, axis=0, keepdims=True)
        cols[GROUP_COL[g]] = cols[GROUP_COL[g]] + left
        cols[GROUP_COL[g] + 1] = cols[GROUP_COL[g] + 1] + (both - left)
    return cols


def row_dot(matrix, row):
    return jnp.sum(matrix * row, axis=1, keepdims=True)


def face_kernel(
    place, live, h_in, h_n, h_s, h_w, h_e, q_n, q_s, q_w, q_e, finv, tmap, r_out, z_out, slots, send,
    a_hi, a_lo, x, p_in, p_n, p_s, p_w, p_e, sems
):
    sources = (h_in, h_n, h_s, h_w, h_e)
    targets = (p_in, p_n, p_s, p_w, p_e)
    copies = [pltpu.make_async_copy(sources[i], targets[i], sems.at[i]) for i in range(5)]
    for copy in copies:
        copy.start()

    def kept(m):
        return (p_n, p_in.at[0], p_s, p_w.at[0], p_w.at[1], p_e.at[0], p_e.at[1])[m]

    def alive(m):
        return (live[0], 1.0, live[1], live[2], live[2], live[3], live[3])[m]

    def own_part(m, start_, count):
        return kept(m)[start_ : start_ + count, :]

    def other_part(m, start_, count):
        if m == 1:
            return p_in[1, NF + start_ : NF + start_ + count, :]
        if m in (0, 2):
            at = HALF + start_
            return (q_n if m == 0 else q_s)[at : at + count, :]
        side = q_w if m < 5 else q_e
        which = (m - 3) % 2
        at = NF + NCOR * which if start_ == 0 else NF + 2 * NCOR + 2 * which + start_ - NCOR
        return side[at : at + count, :]

    def one_square(q):
        row, col = iota((HALF, HALF), 0), iota((HALF, HALF), 1)
        square = q[0:HALF, 0:HALF]
        low = q[0:HALF, HALF:]
        turned = jnp.transpose(square)
        line = q[HALF + NCOR + 2 : HALF + NCOR + 3, 0:HALF]
        upper = jnp.where(row > col, square, jnp.where(row < col, turned, line))
        lower = jnp.where(row > col, turned, square)
        return jnp.concatenate(
            [jnp.concatenate([upper, jnp.transpose(low)], axis=1), jnp.concatenate([low, lower], axis=1)], axis=0
        )

    def two_squares(q):
        row, col = iota((NF, NF), 0), iota((NF, NF), 1)
        square = q[0:NF, :]
        turned = jnp.transpose(square)
        line = q[NF + 2 * NCOR + 4 : NF + 2 * NCOR + 5, :]
        return (
            jnp.where(row > col, square, jnp.where(row < col, turned, line)),
            jnp.where(row > col, turned, square),
        )

    received = {0: one_square(q_n), 2: one_square(q_s)}
    received[3], received[4] = two_squares(q_w)
    received[5], received[6] = two_squares(q_e)
    for m, block in received.items():
        x[m] = block
    for copy in copies:
        copy.wait()
    eye = jnp.where(iota((NF, NF), 0) == iota((NF, NF), 1), 1.0, 0.0)
    guess = []
    for m in range(7):
        full = own_part(m, 0, NF) + (p_in[1, 0:NF, :] if m == 1 else x[m])
        hi, lo = split2(full)
        a_hi[m] = hi
        a_lo[m] = lo
        size = jnp.max(jnp.sum(jnp.abs(full), axis=0, keepdims=True))
        scale = 1.9 / size
        guess.append(scale)
        x[m] = scale * (2.0 * eye - scale * full)

    def rough(state):
        count, _ = state
        worst = jnp.float32(0.0)
        for m in range(7):
            now = x[m]
            near = now.astype(BF16)
            left = eye - nn(a_hi[m], near)
            worst = jnp.maximum(worst, jnp.sum(left * left))
            x[m] = now + nn(near, left.astype(BF16))
        return count + 1, worst

    def rough_on(state):
        count, worst = state
        return jnp.logical_and(count < 24, jnp.logical_not(worst < 0.1))

    _, worst = lax.while_loop(rough_on, rough, (jnp.int32(0), jnp.float32(1e9)))
    fine_start = worst < 0.1

    @pl.when(jnp.logical_not(fine_start))
    def _():
        for m in range(7):
            x[m] = guess[m] * eye

    def fine(state):
        count, _ = state
        worst = jnp.float32(0.0)
        for m in range(7):
            now = x[m]
            hi, lo = split2(now)
            left = eye - (nn(a_hi[m], hi) + (nn(a_hi[m], lo) + nn(a_lo[m], hi)))
            worst = jnp.maximum(worst, jnp.sum(left * left))
            x[m] = now + nn(hi, left.astype(BF16))
        return count + 1, worst

    def fine_on(state):
        count, worst = state
        return jnp.logical_and(count < 60, jnp.logical_not(worst < 1e-3))

    lax.while_loop(fine_on, fine, (jnp.int32(0), jnp.float32(1e9)))

    gathered = {}

    def gather(g, value):
        gathered[g] = value if g not in gathered else gathered[g] + value

    rows_r = []
    rows_i = [None] * 8
    for m in range(7):
        inverse = x[m] * alive(m)
        finv[m] = inverse
        both = jnp.concatenate([own_part(m, NF, NCOR), other_part(m, 0, NCOR)], axis=0)
        b_hi, b_lo = split2(both)
        i_hi, i_lo = split2(inverse)
        lifted = nn(jnp.concatenate([b_hi, b_lo], axis=0), i_hi)
        mapped = lifted[:48] + lifted[48:] + nn(b_hi, i_lo)
        tmap[m] = mapped
        resid = alive(m) * (own_part(m, NF + NCOR, 1) + other_part(m, NCOR, 1))
        rows_r.append(resid)
        gather(GROUPS[m][0], row_dot(mapped[:NCOR], resid))
        if m == 1:
            gather(GROUPS[m][1], row_dot(mapped[NCOR:], resid))
        rows_i[GROUPS[m][0]] = own_part(m, NF + NCOR + 1, 1)[:, 0:128]
        rows_i[GROUPS[m][1]] = other_part(m, NCOR + 1, 1)[:, 0:128]
    resid = jnp.concatenate(rows_r + [jnp.zeros((1, NF), F32)], axis=0)
    r_out[...] = resid
    z_out[...] = face_apply(finv, resid)
    numbers = jnp.transpose(jnp.concatenate(rows_i, axis=0))[:NCOR, :]
    slots[...] = numbers
    sums = spread_window(gathered)
    upper = iota((NCOR, 1), 0) < 12
    named = {0: jnp.where(upper, numbers[:, 0:1] + 1.0, 0.0)}
    keep = jnp.logical_or(upper, place[0] == GRID_X - 1)
    named[1] = jnp.where(keep, numbers[:, 1:2] + 1.0, 0.0)
    names = spread_window(named)
    edge = jnp.where(place[1] == GRID_Y - 1, names[2], 0.0)
    send[...] = jnp.broadcast_to(jnp.concatenate([sums[1], sums[2], names[1], edge], axis=1), (DEV, 128))


def face_apply(finv, rows):
    turned = jnp.transpose(rows)
    outs = [jnp.sum(finv[m] * turned[:, m : m + 1], axis=0, keepdims=True) for m in range(7)]
    return jnp.concatenate(outs + [jnp.zeros((1, NF), F32)], axis=0)


def smem():
    return pl.BlockSpec(memory_space=pltpu.SMEM)


def vmem():
    return pl.BlockSpec(memory_space=pltpu.VMEM)


def faces(place, live, *packets):
    return pl.pallas_call(
        face_kernel,
        in_specs=[smem(), smem()] + [pl.BlockSpec(memory_space=pl.ANY)] * 5 + [vmem()] * 4,
        out_shape=[
            jax.ShapeDtypeStruct((7, NF, NF), F32),
            jax.ShapeDtypeStruct((7, 48, NF), F32),
            jax.ShapeDtypeStruct((8, NF), F32),
            jax.ShapeDtypeStruct((8, NF), F32),
            jax.ShapeDtypeStruct((NCOR, 8), F32),
            jax.ShapeDtypeStruct((DEV, 128), F32),
        ],
        scratch_shapes=[
            pltpu.VMEM((7, NF, NF), BF16),
            pltpu.VMEM((7, NF, NF), BF16),
            pltpu.VMEM((7, NF, NF), F32),
            pltpu.VMEM((2, PKT, NF), F32),
            pltpu.VMEM((PKT, NF), F32),
            pltpu.VMEM((PKT, NF), F32),
            pltpu.VMEM((2, PKT, NF), F32),
            pltpu.VMEM((2, PKT, NF), F32),
            pltpu.SemaphoreType.DMA((5,)),
        ],
        compiler_params=pltpu.CompilerParams(vmem_limit_bytes=16 * 2**20),
        cost_estimate=pl.CostEstimate(flops=5 * 10**9, transcendentals=0, bytes_accessed=10 * 2**20),
        name="faces",
    )(place, live, *packets)


def total_columns(got):
    lane = iota((GRID_Y, 128), 1)
    totals = [None] * 4
    for ix in range(GRID_X):
        part = got[ix * GRID_Y : (ix + 1) * GRID_Y, :]
        for v in range(4):
            inside = jnp.logical_and(lane >= 32 * v, lane < 32 * v + 30)
            moved = pltpu.roll(jnp.where(inside, part, 0.0), (12 * ix - 6 - 32 * v) % 128, 1)
            totals[v] = moved if totals[v] is None else totals[v] + moved
    return totals


def owner_line(inverse, grid):
    partial = jnp.zeros((16, 128), F32)
    for col in range(1, 18):
        partial = partial + inverse[col] * grid[col : col + 1, :]
    column = jnp.sum(partial, axis=1, keepdims=True)
    return jnp.sum(jnp.where(iota((16, 128), 0) == iota((16, 128), 1), column, 0.0), axis=0, keepdims=True)


def start_kernel(got, columns, inverse, out, grid, table, padded):
    totals = total_columns(got)
    grid[...] = jnp.zeros((VC, 128), F32)
    grid[1:17, :] = totals[0]
    grid[2:18, :] = grid[2:18, :] + totals[1]
    table[1:17, :] = totals[2]
    table[17:18, :] = totals[3][GRID_Y - 1 : GRID_Y, :]
    padded[...] = jnp.zeros((16, NCOARSE), F32)
    padded[0:OWN, :] = columns[...]
    lhs = jnp.concatenate(split3(padded[...]), axis=0)
    rows = iota((NCOARSE, 256), 0) + 1
    for pair in range(9):
        first_ = table[2 * pair + 1 : 2 * pair + 2, :]
        second_ = table[2 * pair + 2 : 2 * pair + 3, :] if pair < 8 else jnp.zeros((1, 128), F32)
        wanted = jnp.concatenate([first_, second_], axis=1).astype(jnp.int32)
        got_ = nn(lhs, (rows == wanted).astype(BF16))
        got_ = got_[0:16] + got_[16:32] + got_[32:48]
        inverse[2 * pair + 1] = got_[:, :128]
        if pair < 8:
            inverse[2 * pair + 2] = got_[:, 128:]
    for other in (0, *range(18, VC)):
        inverse[other] = jnp.zeros((16, 128), F32)
    out[...] = jnp.broadcast_to(owner_line(inverse, grid), (DEV, 128))


def start(got, columns):
    return pl.pallas_call(
        start_kernel,
        out_shape=[jax.ShapeDtypeStruct((VC, 16, 128), F32), jax.ShapeDtypeStruct((DEV, 128), F32)],
        scratch_shapes=[pltpu.VMEM((VC, 128), F32), pltpu.VMEM((VC, 128), F32), pltpu.VMEM((16, NCOARSE), F32)],
        compiler_params=pltpu.CompilerParams(vmem_limit_bytes=8 * 2**20),
        cost_estimate=pl.CostEstimate(flops=10**9, transcendentals=0, bytes_accessed=2**20),
        name="start",
    )(got, columns)


def owner_kernel(place, live, got, inverse, image, out, sums, grid):
    totals = total_columns(got)
    grid[...] = jnp.zeros((VC, 128), F32)
    for vc in range(4):
        grid[vc : vc + GRID_Y, :] = grid[vc : vc + GRID_Y, :] + totals[vc]
    sums[...] = jnp.broadcast_to(jnp.sum(got[...], axis=0, keepdims=True), (8, 128))
    out[:, 0:128] = jnp.broadcast_to(owner_line(inverse, grid), (DEV, 128))
    out[:, 128:] = jnp.zeros((DEV, 512), F32)
    post(place, live, image, out)


def owners(place, live, got, inverse, image):
    return pl.pallas_call(
        owner_kernel,
        in_specs=[smem(), smem()] + [vmem()] * 3,
        out_shape=[jax.ShapeDtypeStruct((DEV, 640), F32), jax.ShapeDtypeStruct((8, 128), F32)],
        scratch_shapes=[pltpu.VMEM((VC, 128), F32)],
        compiler_params=pltpu.CompilerParams(vmem_limit_bytes=6 * 2**20),
        cost_estimate=pl.CostEstimate(flops=10**6, transcendentals=0, bytes_accessed=2**20),
        name="owners",
    )(place, live, got, inverse, image)


def coarse_values(slots, coarse):
    lane = iota((NCOR, 128), 1).astype(F32)
    owner_rows = []
    places = []
    for g in range(8):
        number = slots[:, g : g + 1]
        owner = jnp.floor((number + 0.5) * (1.0 / OWN))
        places.append(number - OWN * owner)
        owner_rows.append(jnp.where(lane == owner, 1.0, 0.0))
    picked = lax.dot_general(
        jnp.concatenate(owner_rows, axis=0),
        coarse[:, 0:128],
        (((1,), (0,)), ((), ())),
        precision=HIGHEST,
        preferred_element_type=F32,
    )
    return [
        jnp.sum(jnp.where(lane == places[g], picked[g * NCOR : (g + 1) * NCOR], 0.0), axis=1, keepdims=True)
        for g in range(8)
    ]


def prolong(tmap, values):
    outs = []
    for m in range(7):
        column = jnp.concatenate([values[GROUPS[m][0]], values[GROUPS[m][1]]], axis=0)
        outs.append(jnp.sum(tmap[m] * column, axis=0, keepdims=True))
    return jnp.concatenate(outs + [jnp.zeros((1, NF), F32)], axis=0)


def subdomain_apply(s_ref, vector):
    turned = jnp.transpose(vector)
    rows = []
    for s in range(2):
        across = [None] * 4
        upright = [None] * 4
        for f in range(4):
            column = turned[:, FACE[s][f] : FACE[s][f] + 1]
            for g in range(f, 4):
                block = s_ref[s, BLOCK[f, g]].astype(F32)
                down = jnp.sum(block * column, axis=0, keepdims=True)
                across[g] = down if across[g] is None else across[g] + down
                if g > f:
                    m = FACE[s][g]
                    side = row_dot(block, vector[m : m + 1, :])
                    upright[f] = side if upright[f] is None else upright[f] + side
        columns = jnp.concatenate(
            [jnp.broadcast_to(upright[f], (NF, 128)) if f < 3 else jnp.zeros((NF, 128), F32) for f in range(4)], axis=1
        )
        lane_pick = jnp.concatenate([columns[:, f * 128 : f * 128 + 1] for f in range(4)] * 2, axis=1)
        flipped = jnp.transpose(lane_pick)
        for f in range(4):
            rows.append(across[f] + flipped[f : f + 1, :])
    return jnp.concatenate(rows, axis=0)


def restrict(tmap, image):
    gathered = {}

    def gather(g, value):
        gathered[g] = value if g not in gathered else gathered[g] + value

    for m in range(7):
        line = None
        for s in range(2):
            for f in range(4):
                if FACE[s][f] == m:
                    row = image[s * 4 + f : s * 4 + f + 1, :]
                    line = row if line is None else line + row
        gather(GROUPS[m][0], row_dot(tmap[m, 0:NCOR], line))
        gather(GROUPS[m][1], row_dot(tmap[m, NCOR:], line))
    return spread_window(gathered)


def post(place, live, image, send):
    me = place[0] * GRID_Y + place[1]

    def put(target, slot, row):
        at = pl.ds(target, 1)
        send[at, slot * 128 : slot * 128 + NF] = image[row : row + 1, :]

    @pl.when(live[0] > 0.0)
    def _():
        put(me - GRID_Y, 1, 0)

    @pl.when(live[1] > 0.0)
    def _():
        put(me + GRID_Y, 1, 5)

    @pl.when(live[2] > 0.0)
    def _():
        put(me - 1, 1, 2)
        put(me - 1, 3, 6)

    @pl.when(live[3] > 0.0)
    def _():
        put(me + 1, 1, 3)
        put(me + 1, 3, 7)


def meet(place, live, image, got):
    me = place[0] * GRID_Y + place[1]

    def read(source, slot, alive):
        at = jnp.clip(source, 0, DEV - 1)
        row = got[pl.ds(at, 1), slot * 128 : slot * 128 + NF]
        return jnp.where(alive > 0.0, row, 0.0)

    def mine(row):
        return image[row : row + 1, :]

    return jnp.concatenate(
        [
            live[0] * (mine(0) + read(me - GRID_Y, 1, live[0])),
            mine(1) + mine(4),
            live[1] * (mine(5) + read(me + GRID_Y, 1, live[1])),
            live[2] * (mine(2) + read(me - 1, 1, live[2])),
            live[2] * (mine(6) + read(me - 1, 3, live[2])),
            live[3] * (mine(3) + read(me + 1, 1, live[3])),
            live[3] * (mine(7) + read(me + 1, 3, live[3])),
            jnp.zeros((1, NF), F32),
        ],
        axis=0,
    )


def shared_dot(first, second):
    weight = jnp.where(iota((8, NF), 0) == 1, 1.0, 0.5)
    return jnp.sum(weight * first * second)


def sides(vector):
    return jnp.concatenate([vector[m : m + 1, :] for s in range(2) for m in FACE[s]], axis=0)


def tag(row, *scalars):
    lane = iota((1, 128), 1)
    for at, value in scalars:
        row = jnp.where(lane == at, value, row)
    return row


def first_kernel(place, live, s_ref, tmap, resid, smooth, slots, coarse, z_out, c_out, send):
    z = smooth[...] + prolong(tmap, coarse_values(slots, coarse))
    z_out[...] = z
    image = subdomain_apply(s_ref, z)
    c_out[...] = image
    cols = restrict(tmap, image)
    gamma = shared_dot(resid[...], z)
    delta = jnp.sum(sides(z) * image)
    line = tag(jnp.concatenate(cols, axis=1), (30, gamma), (31, delta))
    send[...] = jnp.broadcast_to(line, (DEV, 128))


def first(place, live, *rest):
    return pl.pallas_call(
        first_kernel,
        in_specs=[smem(), smem()] + [vmem()] * 6,
        out_shape=[
            jax.ShapeDtypeStruct((8, NF), F32),
            jax.ShapeDtypeStruct((8, NF), F32),
            jax.ShapeDtypeStruct((DEV, 128), F32),
        ],
        compiler_params=pltpu.CompilerParams(vmem_limit_bytes=10 * 2**20),
        cost_estimate=pl.CostEstimate(flops=10**7, transcendentals=0, bytes_accessed=10 * 2**20),
        name="first",
    )(place, live, *rest)


def pick_lane(row, at):
    return jnp.sum(jnp.where(iota((1, 128), 1) == at, row, 0.0))


def second_kernel(place, live, s_ref, finv, tmap, resid, z_old, c_old, slots, sums, got, z_out, c_out, w_out, r_out, send):
    gamma = pick_lane(sums[0:1, :], 30)
    delta = pick_lane(sums[0:1, :], 31)
    alpha = gamma / delta
    w = meet(place, live, c_old, got)
    w_out[...] = w
    y = face_apply(finv, w) + prolong(tmap, coarse_values(slots, got))
    z = z_old[...] - alpha * y
    r = resid[...] - alpha * w
    z_out[...] = z
    r_out[...] = r
    image = subdomain_apply(s_ref, z)
    c_out[...] = image
    gamma_new = shared_dot(r, z)
    new_new = jnp.sum(sides(z) * image)
    old_new = jnp.sum(sides(z_old[...]) * image)
    new_old = jnp.sum(sides(z) * c_old[...])
    line = tag(
        jnp.zeros((1, 128), F32), (0, gamma_new), (1, new_new), (2, old_new), (3, new_old)
    )
    send[:, 0:128] = jnp.broadcast_to(line, (DEV, 128))
    send[:, 128:] = jnp.zeros((DEV, 512), F32)
    post(place, live, image, send)


def second(place, live, *rest):
    small = jax.ShapeDtypeStruct((8, NF), F32)
    return pl.pallas_call(
        second_kernel,
        in_specs=[smem(), smem()] + [vmem()] * 9,
        out_shape=[small, small, small, small, jax.ShapeDtypeStruct((DEV, 640), F32)],
        compiler_params=pltpu.CompilerParams(vmem_limit_bytes=14 * 2**20),
        cost_estimate=pl.CostEstimate(flops=10**7, transcendentals=0, bytes_accessed=12 * 2**20),
        name="second",
    )(place, live, *rest)


def last_kernel(place, live, z_old, w_old, z_new, c_new, resid, sums, got, x_out, r_out):
    line = jnp.sum(got[:, 0:128], axis=0, keepdims=True)
    gamma = pick_lane(sums[0:1, :], 30)
    delta = pick_lane(sums[0:1, :], 31)
    alpha = gamma / delta
    gamma_new = pick_lane(line, 0)
    beta = gamma_new / gamma
    curve = pick_lane(line, 1) + beta * (pick_lane(line, 2) + pick_lane(line, 3)) + beta * beta * delta
    alpha_new = gamma_new / curve
    w = meet(place, live, c_new[...], got)
    search = z_new[...] + beta * z_old[...]
    along = w + beta * w_old[...]
    x = sides(alpha * z_old[...] + alpha_new * search)
    r = sides(resid[...] - alpha_new * along)
    for s in range(2):
        x_out[s, 0] = x[4 * s : 4 * s + 4]
        r_out[s, 0] = r[4 * s : 4 * s + 4]


def last(place, live, *rest):
    out = jax.ShapeDtypeStruct((2, 1, 4, NF), F32)
    return pl.pallas_call(
        last_kernel,
        in_specs=[smem(), smem()] + [vmem()] * 7,
        out_shape=[out, out],
        compiler_params=pltpu.CompilerParams(vmem_limit_bytes=6 * 2**20),
        cost_estimate=pl.CostEstimate(flops=10**6, transcendentals=0, bytes_accessed=2**20),
        name="last",
    )(place, live, *rest)


def shift(value, axis, steps):
    count = lax.axis_size(axis)
    first_, last_ = max(0, -steps), min(count, count - steps)
    return lax.ppermute(value, axis, [(source, source + steps) for source in range(first_, last_)])


def exchange(packet):
    return lax.all_to_all(packet, GX_GY, 0, 0, tiled=True)


def shards(inverse, couple, stiff, basis, loads, order, corner_index, coarse_inverse):
    ix = lax.axis_index(GX)
    iy = lax.axis_index(GY)
    place = jnp.stack([ix, iy]).astype(jnp.int32)
    live = jnp.stack([ix > 0, ix < GRID_X - 1, iy > 0, iy < GRID_Y - 1]).astype(F32)
    s_full, p_in, p_n, p_s, p_w, p_e, t_n, t_s, t_w, t_e = schur(order, inverse, couple, stiff, basis, loads, corner_index)
    q_s = shift(t_n, GX, -1)
    q_n = shift(t_s, GX, 1)
    q_e = shift(t_w, GY, -1)
    q_w = shift(t_e, GY, 1)
    finv, tmap, resid, smooth, slots, send = faces(
        place, live, *(pltpu.with_memory_space_constraint(p, pltpu.HBM) for p in (p_in, p_n, p_s, p_w, p_e)), q_n, q_s, q_w, q_e
    )
    coarse, values = start(exchange(send), jnp.transpose(coarse_inverse))
    z0, c0, send = first(place, live, s_full, tmap, resid, smooth, slots, exchange(values))
    send, sums = owners(place, live, exchange(send), coarse, c0)
    z1, c1, w0, r1, send = second(place, live, s_full, finv, tmap, resid, z0, c0, slots, sums, exchange(send))
    return tuple(last(place, live, z0, w0, z1, c1, r1, sums, exchange(send)))


def solution(mesh):
    torus = Mesh(mesh.devices.reshape(4, 2, 4, 2, 2), GX_GY)
    in_specs = (
        P(GX, GY, None, None),
        P(GX, GY, None, None),
        P(GX, GY, None, None, None),
        P(GX, GY, None, None),
        P(GX, GY, None, None),
        P(GX, GY, None, None),
        P(GX, GY, None),
        P(None, GX_GY),
    )
    out_specs = (P(GX, GY, None, None), P(GX, GY, None, None))
    return jax.shard_map(shards, mesh=torus, in_specs=in_specs, out_specs=out_specs, check_vma=False)
```

```python
import jax
import jax.numpy as jnp
from jax import lax
from jax.experimental import pallas as pl
from jax.experimental.pallas import tpu as pltpu
from jax.sharding import Mesh
from jax.sharding import PartitionSpec as P

GX = ("gx_0", "gx_1")
GY = ("gy_0", "gy_1", "gy_2")
GX_GY = GX + GY

NI = 1536
NF = 256
NCOR = 24
NCOARSE = 1792
OWN = 14
GRID_X = 8
GRID_Y = 16
DEV = 128
PKT = 288
ONE = 160
TWO = 312
HALF = NF // 2
STEPS = 2
CHUNK = NI // STEPS
VC = 24
F32 = jnp.float32
BF16 = jnp.bfloat16
HIGHEST = lax.Precision.HIGHEST

FACE = ((0, 1, 3, 5), (1, 2, 4, 6))
GROUPS = ((0, 2), (0, 1), (1, 3), (0, 4), (1, 5), (0, 6), (1, 7))
GROUP_ROW = (0, 1, -1, 2, 0, 1, 0, 1)
GROUP_COL = (1, 1, 1, 1, 0, 0, 2, 2)


def nn(a, b):
    return lax.dot_general(a, b, (((1,), (0,)), ((), ())), preferred_element_type=F32)


def nt(a, b):
    return lax.dot_general(a, b, (((1,), (1,)), ((), ())), preferred_element_type=F32)


def split2(x):
    hi = x.astype(BF16)
    return hi, (x - hi.astype(F32)).astype(BF16)


def split3(x):
    hi = x.astype(BF16)
    rest = x - hi.astype(F32)
    mid = rest.astype(BF16)
    return hi, mid, (rest - mid.astype(F32)).astype(BF16)


def iota(shape, dim):
    return lax.broadcasted_iota(jnp.int32, shape, dim)


BLOCK = {}
for f_ in range(4):
    for g_ in range(f_, 4):
        BLOCK[f_, g_] = len(BLOCK)


def schur_kernel(order, inverse, couple, stiff, basis, loads, index, s_out, p_in, p_n, p_s, p_w, p_e, t_n, t_s, t_w, t_e, ct, prod, pick):
    sub = pl.program_id(0)
    step = pl.program_id(1)

    @pl.when(step == 0)
    def _():
        for f in range(4):
            chosen = (iota((NF, NF), 0) == order[f : f + 1, :]).astype(BF16)
            pick[f] = chosen
            ct[f * NF : (f + 1) * NF, :] = nt(chosen, couple[:, f * NF : (f + 1) * NF]).astype(BF16)

    prod[pl.ds(step * CHUNK, CHUNK), :] = nt(inverse[...], ct[...]).astype(BF16)

    @pl.when(step == STEPS - 1)
    def _():
        for f in range(4):
            rows = slice(f * NF, (f + 1) * NF)
            back = nn(ct[rows, :], prod[:, f * NF :])
            chosen = pick[f]
            canon = nt(nn(chosen, stiff[f]).astype(BF16), chosen)
            diag = canon - back[:, :NF]
            s_out[BLOCK[f, f]] = diag.astype(BF16)
            for g in range(f + 1, 4):
                s_out[BLOCK[f, g]] = (-back[:, (g - f) * NF : (g - f + 1) * NF]).astype(BF16)
            lowered = nt(basis[:, f * NF : (f + 1) * NF], chosen).astype(BF16)
            hi, lo = split2(diag)
            corner = nn(lowered, hi) + nn(lowered, lo)
            parts = jnp.concatenate(
                [part.astype(F32) for part in split3(jnp.broadcast_to(loads[f : f + 1, :], (8, NF)))], axis=0
            ).astype(BF16)
            placed = nt(parts, chosen)
            load = placed[0:8] + placed[8:16] + placed[16:24]

            def put(out, lead):
                out[lead + (slice(0, NF), slice(None))] = diag
                out[lead + (slice(NF, NF + NCOR), slice(None))] = corner
                out[lead + (slice(NF + NCOR, NF + NCOR + 8), slice(None))] = jnp.where(iota((8, NF), 0) == 0, load, 0.0)
                out[lead + (slice(NF + NCOR + 1, NF + NCOR + 2), slice(0, NCOR))] = index[...].astype(F32)

            def put_one(out):
                row, col = iota((HALF, HALF), 0), iota((HALF, HALF), 1)
                first_ = diag[:HALF, :HALF]
                out[0:HALF, 0:HALF] = jnp.where(row > col, first_, diag[HALF:, HALF:])
                out[0:HALF, HALF:] = diag[HALF:, :HALF]
                out[HALF : HALF + NCOR, :] = corner
                at = HALF + NCOR
                out[at : at + 8, :] = jnp.where(iota((8, NF), 0) == 0, load, 0.0)
                out[at + 1 : at + 2, 0:NCOR] = index[...].astype(F32)
                out[at + 2 : at + 3, 0:HALF] = jnp.sum(jnp.where(row == col, first_, 0.0), axis=0, keepdims=True)

            def put_two(out, kept):
                row, col = iota((NF, NF), 0), iota((NF, NF), 1)
                first_ = kept[0, 0:NF, :]
                out[0:NF, :] = jnp.where(row > col, first_, diag)
                out[NF : NF + NCOR, :] = kept[0, NF : NF + NCOR, :]
                out[NF + NCOR : NF + 2 * NCOR, :] = corner
                at = NF + 2 * NCOR
                out[at : at + 8, :] = jnp.where(iota((8, NF), 0) == 2, load, 0.0)
                out[at : at + 2, :] = kept[0, NF + NCOR : NF + NCOR + 2, :]
                out[at + 3 : at + 4, 0:NCOR] = index[...].astype(F32)
                out[at + 4 : at + 5, :] = jnp.sum(jnp.where(row == col, first_, 0.0), axis=0, keepdims=True)

            def both(*steps):
                def run():
                    for one in steps:
                        one()

                return run

            if f == 0:
                pl.when(sub == 0)(both(lambda: put(p_n, ()), lambda: put_one(t_n)))
                pl.when(sub == 1)(lambda: put(p_in, (1,)))
            elif f == 1:
                pl.when(sub == 0)(lambda: put(p_in, (0,)))
                pl.when(sub == 1)(both(lambda: put(p_s, ()), lambda: put_one(t_s)))
            else:
                kept, out_ = (p_w, t_w) if f == 2 else (p_e, t_e)
                pl.when(sub == 0)(lambda: put(kept, (0,)))
                pl.when(sub == 1)(both(lambda: put(kept, (1,)), lambda: put_two(out_, kept)))


def schur(order, inverse, couple, stiff, basis, loads, index):
    pkt = pltpu.HBM((PKT, NF), F32)
    pair = pltpu.HBM((2, PKT, NF), F32)
    one = jax.ShapeDtypeStruct((ONE, NF), F32)
    two = jax.ShapeDtypeStruct((TWO, NF), F32)
    return pl.pallas_call(
        schur_kernel,
        grid=(2, STEPS),
        in_specs=[
            pl.BlockSpec((None, None, 4, NF), lambda s, j: (s, 0, 0, 0)),
            pl.BlockSpec((None, None, CHUNK, NI), lambda s, j: (s, 0, j, 0)),
            pl.BlockSpec((None, None, NI, 4 * NF), lambda s, j: (s, 0, 0, 0)),
            pl.BlockSpec((None, None, 4, NF, NF), lambda s, j: (s, 0, 0, 0, 0)),
            pl.BlockSpec((None, None, NCOR, 4 * NF), lambda s, j: (s, 0, 0, 0)),
            pl.BlockSpec((None, None, 4, NF), lambda s, j: (s, 0, 0, 0)),
            pl.BlockSpec((None, 1, NCOR), lambda s, j: (s, 0, 0)),
        ],
        out_specs=[
            pl.BlockSpec((None, 10, NF, NF), lambda s, j: (s, 0, 0, 0)),
            pl.BlockSpec((2, PKT, NF), lambda s, j: (0, 0, 0)),
            pl.BlockSpec((PKT, NF), lambda s, j: (0, 0)),
            pl.BlockSpec((PKT, NF), lambda s, j: (0, 0)),
            pl.BlockSpec((2, PKT, NF), lambda s, j: (0, 0, 0)),
            pl.BlockSpec((2, PKT, NF), lambda s, j: (0, 0, 0)),
            pl.BlockSpec((ONE, NF), lambda s, j: (0, 0)),
            pl.BlockSpec((ONE, NF), lambda s, j: (0, 0)),
            pl.BlockSpec((TWO, NF), lambda s, j: (0, 0)),
            pl.BlockSpec((TWO, NF), lambda s, j: (0, 0)),
        ],
        out_shape=[jax.ShapeDtypeStruct((2, 10, NF, NF), BF16), pair, pkt, pkt, pair, pair, one, one, two, two],
        scratch_shapes=[
            pltpu.VMEM((4 * NF, NI), BF16),
            pltpu.VMEM((NI, 4 * NF), BF16),
            pltpu.VMEM((4, NF, NF), BF16),
        ],
        compiler_params=pltpu.CompilerParams(
            dimension_semantics=("arbitrary", "arbitrary"), vmem_limit_bytes=40 * 2**20
        ),
        cost_estimate=pl.CostEstimate(flops=16 * 10**9, transcendentals=0, bytes_accessed=32 * 2**20),
        name="schur",
    )(*(pltpu.with_memory_space_constraint(x, pltpu.HBM) for x in (order, inverse, couple, stiff, basis, loads, index)))


def spread_window(contributions):
    corner = iota((NCOR, 32), 0)
    lane = iota((NCOR, 32), 1)
    below = jnp.where(corner >= 12, 1, 0)
    inside = corner - 12 * below
    right = inside >= 6
    dof = inside - jnp.where(right, 6, 0)
    cols = [jnp.zeros((1, 32), F32) for _ in range(4)]
    for g, value in contributions.items():
        target = (GROUP_ROW[g] + 1 + below) * 6 + dof
        filled = jnp.where(lane == target, jnp.broadcast_to(value, (NCOR, 32)), 0.0)
        left = jnp.sum(jnp.where(right, 0.0, filled), axis=0, keepdims=True)
        both = jnp.sum(filled, axis=0, keepdims=True)
        cols[GROUP_COL[g]] = cols[GROUP_COL[g]] + left
        cols[GROUP_COL[g] + 1] = cols[GROUP_COL[g] + 1] + (both - left)
    return cols


def row_dot(matrix, row):
    return jnp.sum(matrix * row, axis=1, keepdims=True)


def face_kernel(
    place, live, h_in, h_n, h_s, h_w, h_e, q_n, q_s, q_w, q_e, finv, tmap, r_out, z_out, slots, send,
    a_hi, a_lo, x, p_in, p_n, p_s, p_w, p_e, sems
):
    sources = (h_in, h_n, h_s, h_w, h_e)
    targets = (p_in, p_n, p_s, p_w, p_e)
    copies = [pltpu.make_async_copy(sources[i], targets[i], sems.at[i]) for i in range(5)]
    for copy in copies:
        copy.start()

    def kept(m):
        return (p_n, p_in.at[0], p_s, p_w.at[0], p_w.at[1], p_e.at[0], p_e.at[1])[m]

    def alive(m):
        return (live[0], 1.0, live[1], live[2], live[2], live[3], live[3])[m]

    def own_part(m, start_, count):
        return kept(m)[start_ : start_ + count, :]

    def other_part(m, start_, count):
        if m == 1:
            return p_in[1, NF + start_ : NF + start_ + count, :]
        if m in (0, 2):
            at = HALF + start_
            return (q_n if m == 0 else q_s)[at : at + count, :]
        side = q_w if m < 5 else q_e
        which = (m - 3) % 2
        at = NF + NCOR * which if start_ == 0 else NF + 2 * NCOR + 2 * which + start_ - NCOR
        return side[at : at + count, :]

    def one_square(q):
        row, col = iota((HALF, HALF), 0), iota((HALF, HALF), 1)
        square = q[0:HALF, 0:HALF]
        low = q[0:HALF, HALF:]
        turned = jnp.transpose(square)
        line = q[HALF + NCOR + 2 : HALF + NCOR + 3, 0:HALF]
        upper = jnp.where(row > col, square, jnp.where(row < col, turned, line))
        lower = jnp.where(row > col, turned, square)
        return jnp.concatenate(
            [jnp.concatenate([upper, jnp.transpose(low)], axis=1), jnp.concatenate([low, lower], axis=1)], axis=0
        )

    def two_squares(q):
        row, col = iota((NF, NF), 0), iota((NF, NF), 1)
        square = q[0:NF, :]
        turned = jnp.transpose(square)
        line = q[NF + 2 * NCOR + 4 : NF + 2 * NCOR + 5, :]
        return (
            jnp.where(row > col, square, jnp.where(row < col, turned, line)),
            jnp.where(row > col, turned, square),
        )

    received = {0: one_square(q_n), 2: one_square(q_s)}
    received[3], received[4] = two_squares(q_w)
    received[5], received[6] = two_squares(q_e)
    for m, block in received.items():
        x[m] = block
    for copy in copies:
        copy.wait()
    eye = jnp.where(iota((NF, NF), 0) == iota((NF, NF), 1), 1.0, 0.0)
    guess = []
    for m in range(7):
        full = own_part(m, 0, NF) + (p_in[1, 0:NF, :] if m == 1 else x[m])
        hi, lo = split2(full)
        a_hi[m] = hi
        a_lo[m] = lo
        size = jnp.max(jnp.sum(jnp.abs(full), axis=0, keepdims=True), axis=1, keepdims=True)
        scale = 1.9 / size
        guess.append(scale)
        x[m] = scale * (2.0 * eye - scale * full)

    def square_sum(left):
        return jnp.sum(jnp.sum(left * left, axis=0, keepdims=True), axis=1, keepdims=True)

    def rough(state):
        count, _ = state
        worst = jnp.zeros((1, 1), F32)
        for m in range(7):
            now = x[m]
            near = now.astype(BF16)
            left = eye - nn(a_hi[m], near)
            worst = jnp.maximum(worst, square_sum(left))
            x[m] = now + nn(near, left.astype(BF16))
        return count + 1, jnp.max(worst)

    def rough_on(state):
        count, worst = state
        return jnp.logical_and(count < 24, jnp.logical_not(worst < 0.1))

    _, worst = lax.while_loop(rough_on, rough, (jnp.int32(0), jnp.float32(1e9)))
    fine_start = worst < 0.1

    @pl.when(jnp.logical_not(fine_start))
    def _():
        for m in range(7):
            x[m] = guess[m] * eye

    def fine(state):
        count, _ = state
        worst = jnp.zeros((1, 1), F32)
        for m in range(7):
            now = x[m]
            hi, lo = split2(now)
            left = eye - (nn(a_hi[m], hi) + (nn(a_hi[m], lo) + nn(a_lo[m], hi)))
            worst = jnp.maximum(worst, square_sum(left))
            x[m] = now + nn(hi, left.astype(BF16))
        return count + 1, jnp.max(worst)

    def fine_on(state):
        count, worst = state
        return jnp.logical_and(count < 60, jnp.logical_not(worst < 1e-3))

    lax.while_loop(fine_on, fine, (jnp.int32(0), jnp.float32(1e9)))

    gathered = {}

    def gather(g, value):
        gathered[g] = value if g not in gathered else gathered[g] + value

    rows_r = []
    rows_i = [None] * 8
    for m in range(7):
        inverse = x[m] * alive(m)
        finv[m] = inverse
        both = jnp.concatenate([own_part(m, NF, NCOR), other_part(m, 0, NCOR)], axis=0)
        b_hi, b_lo = split2(both)
        i_hi, i_lo = split2(inverse)
        lifted = nn(jnp.concatenate([b_hi, b_lo], axis=0), i_hi)
        mapped = lifted[:48] + lifted[48:] + nn(b_hi, i_lo)
        tmap[m] = mapped
        resid = alive(m) * (own_part(m, NF + NCOR, 1) + other_part(m, NCOR, 1))
        rows_r.append(resid)
        gather(GROUPS[m][0], row_dot(mapped[:NCOR], resid))
        if m == 1:
            gather(GROUPS[m][1], row_dot(mapped[NCOR:], resid))
        rows_i[GROUPS[m][0]] = own_part(m, NF + NCOR + 1, 1)[:, 0:128]
        rows_i[GROUPS[m][1]] = other_part(m, NCOR + 1, 1)[:, 0:128]
    resid = jnp.concatenate(rows_r + [jnp.zeros((1, NF), F32)], axis=0)
    r_out[...] = resid
    z_out[...] = face_apply(finv, resid)
    numbers = jnp.transpose(jnp.concatenate(rows_i, axis=0))[:NCOR, :]
    slots[...] = numbers
    sums = spread_window(gathered)
    upper = iota((NCOR, 1), 0) < 12
    named = {0: jnp.where(upper, numbers[:, 0:1] + 1.0, 0.0)}
    keep = jnp.logical_or(upper, place[0] == GRID_X - 1)
    named[1] = jnp.where(keep, numbers[:, 1:2] + 1.0, 0.0)
    names = spread_window(named)
    edge = jnp.where(place[1] == GRID_Y - 1, names[2], 0.0)
    send[...] = jnp.broadcast_to(jnp.concatenate([sums[1], sums[2], names[1], edge], axis=1), (DEV, 128))


def face_apply(finv, rows):
    turned = jnp.transpose(rows)
    outs = [jnp.sum(finv[m] * turned[:, m : m + 1], axis=0, keepdims=True) for m in range(7)]
    return jnp.concatenate(outs + [jnp.zeros((1, NF), F32)], axis=0)


def smem():
    return pl.BlockSpec(memory_space=pltpu.SMEM)


def vmem():
    return pl.BlockSpec(memory_space=pltpu.VMEM)


def faces(place, live, *packets):
    return pl.pallas_call(
        face_kernel,
        in_specs=[smem(), smem()] + [pl.BlockSpec(memory_space=pl.ANY)] * 5 + [vmem()] * 4,
        out_shape=[
            jax.ShapeDtypeStruct((7, NF, NF), F32),
            jax.ShapeDtypeStruct((7, 48, NF), F32),
            jax.ShapeDtypeStruct((8, NF), F32),
            jax.ShapeDtypeStruct((8, NF), F32),
            jax.ShapeDtypeStruct((NCOR, 8), F32),
            jax.ShapeDtypeStruct((DEV, 128), F32),
        ],
        scratch_shapes=[
            pltpu.VMEM((7, NF, NF), BF16),
            pltpu.VMEM((7, NF, NF), BF16),
            pltpu.VMEM((7, NF, NF), F32),
            pltpu.VMEM((2, PKT, NF), F32),
            pltpu.VMEM((PKT, NF), F32),
            pltpu.VMEM((PKT, NF), F32),
            pltpu.VMEM((2, PKT, NF), F32),
            pltpu.VMEM((2, PKT, NF), F32),
            pltpu.SemaphoreType.DMA((5,)),
        ],
        compiler_params=pltpu.CompilerParams(vmem_limit_bytes=16 * 2**20),
        cost_estimate=pl.CostEstimate(flops=5 * 10**9, transcendentals=0, bytes_accessed=10 * 2**20),
        name="faces",
    )(place, live, *packets)


def total_columns(got):
    lane = iota((GRID_Y, 128), 1)
    totals = [None] * 4
    for ix in range(GRID_X):
        part = got[ix * GRID_Y : (ix + 1) * GRID_Y, :]
        for v in range(4):
            inside = jnp.logical_and(lane >= 32 * v, lane < 32 * v + 30)
            moved = pltpu.roll(jnp.where(inside, part, 0.0), (12 * ix - 6 - 32 * v) % 128, 1)
            totals[v] = moved if totals[v] is None else totals[v] + moved
    return totals


def owner_line(inverse, grid):
    partial = jnp.zeros((16, 128), F32)
    for col in range(1, 18):
        partial = partial + inverse[col] * grid[col : col + 1, :]
    column = jnp.sum(partial, axis=1, keepdims=True)
    return jnp.sum(jnp.where(iota((16, 128), 0) == iota((16, 128), 1), column, 0.0), axis=0, keepdims=True)


def start_kernel(got, columns, inverse, out, grid, table, padded):
    totals = total_columns(got)
    grid[...] = jnp.zeros((VC, 128), F32)
    grid[1:17, :] = totals[0]
    grid[2:18, :] = grid[2:18, :] + totals[1]
    table[1:17, :] = totals[2]
    table[17:18, :] = totals[3][GRID_Y - 1 : GRID_Y, :]
    padded[...] = jnp.zeros((16, NCOARSE), F32)
    padded[0:OWN, :] = columns[...]
    lhs = jnp.concatenate(split3(padded[...]), axis=0)
    rows = iota((NCOARSE, 256), 0) + 1
    for pair in range(9):
        first_ = table[2 * pair + 1 : 2 * pair + 2, :]
        second_ = table[2 * pair + 2 : 2 * pair + 3, :] if pair < 8 else jnp.zeros((1, 128), F32)
        wanted = jnp.concatenate([first_, second_], axis=1).astype(jnp.int32)
        got_ = nn(lhs, (rows == wanted).astype(BF16))
        got_ = got_[0:16] + got_[16:32] + got_[32:48]
        inverse[2 * pair + 1] = got_[:, :128]
        if pair < 8:
            inverse[2 * pair + 2] = got_[:, 128:]
    for other in (0, *range(18, VC)):
        inverse[other] = jnp.zeros((16, 128), F32)
    out[...] = jnp.broadcast_to(owner_line(inverse, grid), (DEV, 128))


def start(got, columns):
    return pl.pallas_call(
        start_kernel,
        out_shape=[jax.ShapeDtypeStruct((VC, 16, 128), F32), jax.ShapeDtypeStruct((DEV, 128), F32)],
        scratch_shapes=[pltpu.VMEM((VC, 128), F32), pltpu.VMEM((VC, 128), F32), pltpu.VMEM((16, NCOARSE), F32)],
        compiler_params=pltpu.CompilerParams(vmem_limit_bytes=8 * 2**20),
        cost_estimate=pl.CostEstimate(flops=10**9, transcendentals=0, bytes_accessed=2**20),
        name="start",
    )(got, columns)


def owner_kernel(place, live, got, inverse, image, out, sums, grid):
    totals = total_columns(got)
    grid[...] = jnp.zeros((VC, 128), F32)
    for vc in range(4):
        grid[vc : vc + GRID_Y, :] = grid[vc : vc + GRID_Y, :] + totals[vc]
    sums[...] = jnp.broadcast_to(jnp.sum(got[...], axis=0, keepdims=True), (8, 128))
    out[:, 0:128] = jnp.broadcast_to(owner_line(inverse, grid), (DEV, 128))
    out[:, 128:] = jnp.zeros((DEV, 512), F32)
    post(place, live, image, out)


def owners(place, live, got, inverse, image):
    return pl.pallas_call(
        owner_kernel,
        in_specs=[smem(), smem()] + [vmem()] * 3,
        out_shape=[jax.ShapeDtypeStruct((DEV, 640), F32), jax.ShapeDtypeStruct((8, 128), F32)],
        scratch_shapes=[pltpu.VMEM((VC, 128), F32)],
        compiler_params=pltpu.CompilerParams(vmem_limit_bytes=6 * 2**20),
        cost_estimate=pl.CostEstimate(flops=10**6, transcendentals=0, bytes_accessed=2**20),
        name="owners",
    )(place, live, got, inverse, image)


def coarse_values(slots, coarse):
    lane = iota((NCOR, 128), 1).astype(F32)
    owner_rows = []
    places = []
    for g in range(8):
        number = slots[:, g : g + 1]
        owner = jnp.floor((number + 0.5) * (1.0 / OWN))
        places.append(number - OWN * owner)
        owner_rows.append(jnp.where(lane == owner, 1.0, 0.0))
    picked = lax.dot_general(
        jnp.concatenate(owner_rows, axis=0),
        coarse[:, 0:128],
        (((1,), (0,)), ((), ())),
        precision=HIGHEST,
        preferred_element_type=F32,
    )
    return [
        jnp.sum(jnp.where(lane == places[g], picked[g * NCOR : (g + 1) * NCOR], 0.0), axis=1, keepdims=True)
        for g in range(8)
    ]


def prolong(tmap, values):
    outs = []
    for m in range(7):
        column = jnp.concatenate([values[GROUPS[m][0]], values[GROUPS[m][1]]], axis=0)
        outs.append(jnp.sum(tmap[m] * column, axis=0, keepdims=True))
    return jnp.concatenate(outs + [jnp.zeros((1, NF), F32)], axis=0)


def subdomain_apply(s_ref, vector):
    turned = jnp.transpose(vector)
    rows = []
    for s in range(2):
        across = [None] * 4
        upright = [None] * 4
        for f in range(4):
            column = turned[:, FACE[s][f] : FACE[s][f] + 1]
            for g in range(f, 4):
                block = s_ref[s, BLOCK[f, g]].astype(F32)
                down = jnp.sum(block * column, axis=0, keepdims=True)
                across[g] = down if across[g] is None else across[g] + down
                if g > f:
                    m = FACE[s][g]
                    side = row_dot(block, vector[m : m + 1, :])
                    upright[f] = side if upright[f] is None else upright[f] + side
        columns = jnp.concatenate(
            [jnp.broadcast_to(upright[f], (NF, 128)) if f < 3 else jnp.zeros((NF, 128), F32) for f in range(4)], axis=1
        )
        lane_pick = jnp.concatenate([columns[:, f * 128 : f * 128 + 1] for f in range(4)] * 2, axis=1)
        flipped = jnp.transpose(lane_pick)
        for f in range(4):
            rows.append(across[f] + flipped[f : f + 1, :])
    return jnp.concatenate(rows, axis=0)


def restrict(tmap, image):
    gathered = {}

    def gather(g, value):
        gathered[g] = value if g not in gathered else gathered[g] + value

    for m in range(7):
        line = None
        for s in range(2):
            for f in range(4):
                if FACE[s][f] == m:
                    row = image[s * 4 + f : s * 4 + f + 1, :]
                    line = row if line is None else line + row
        gather(GROUPS[m][0], row_dot(tmap[m, 0:NCOR], line))
        gather(GROUPS[m][1], row_dot(tmap[m, NCOR:], line))
    return spread_window(gathered)


def post(place, live, image, send):
    me = place[0] * GRID_Y + place[1]

    def put(target, slot, row):
        at = pl.ds(target, 1)
        send[at, slot * 128 : slot * 128 + NF] = image[row : row + 1, :]

    @pl.when(live[0] > 0.0)
    def _():
        put(me - GRID_Y, 1, 0)

    @pl.when(live[1] > 0.0)
    def _():
        put(me + GRID_Y, 1, 5)

    @pl.when(live[2] > 0.0)
    def _():
        put(me - 1, 1, 2)
        put(me - 1, 3, 6)

    @pl.when(live[3] > 0.0)
    def _():
        put(me + 1, 1, 3)
        put(me + 1, 3, 7)


def meet(place, live, image, got):
    me = place[0] * GRID_Y + place[1]

    def read(source, slot, alive):
        at = jnp.clip(source, 0, DEV - 1)
        row = got[pl.ds(at, 1), slot * 128 : slot * 128 + NF]
        return jnp.where(alive > 0.0, row, 0.0)

    def mine(row):
        return image[row : row + 1, :]

    return jnp.concatenate(
        [
            live[0] * (mine(0) + read(me - GRID_Y, 1, live[0])),
            mine(1) + mine(4),
            live[1] * (mine(5) + read(me + GRID_Y, 1, live[1])),
            live[2] * (mine(2) + read(me - 1, 1, live[2])),
            live[2] * (mine(6) + read(me - 1, 3, live[2])),
            live[3] * (mine(3) + read(me + 1, 1, live[3])),
            live[3] * (mine(7) + read(me + 1, 3, live[3])),
            jnp.zeros((1, NF), F32),
        ],
        axis=0,
    )


def shared_dot(first, second):
    weight = jnp.where(iota((8, NF), 0) == 1, 1.0, 0.5)
    return jnp.sum(weight * first * second)


def sides(vector):
    return jnp.concatenate([vector[m : m + 1, :] for s in range(2) for m in FACE[s]], axis=0)


def tag(row, *scalars):
    lane = iota((1, 128), 1)
    for at, value in scalars:
        row = jnp.where(lane == at, value, row)
    return row


def first_kernel(place, live, s_ref, tmap, resid, smooth, slots, coarse, z_out, c_out, send):
    z = smooth[...] + prolong(tmap, coarse_values(slots, coarse))
    z_out[...] = z
    image = subdomain_apply(s_ref, z)
    c_out[...] = image
    cols = restrict(tmap, image)
    gamma = shared_dot(resid[...], z)
    delta = jnp.sum(sides(z) * image)
    line = tag(jnp.concatenate(cols, axis=1), (30, gamma), (31, delta))
    send[...] = jnp.broadcast_to(line, (DEV, 128))


def first(place, live, *rest):
    return pl.pallas_call(
        first_kernel,
        in_specs=[smem(), smem()] + [vmem()] * 6,
        out_shape=[
            jax.ShapeDtypeStruct((8, NF), F32),
            jax.ShapeDtypeStruct((8, NF), F32),
            jax.ShapeDtypeStruct((DEV, 128), F32),
        ],
        compiler_params=pltpu.CompilerParams(vmem_limit_bytes=10 * 2**20),
        cost_estimate=pl.CostEstimate(flops=10**7, transcendentals=0, bytes_accessed=10 * 2**20),
        name="first",
    )(place, live, *rest)


def pick_lane(row, at):
    return jnp.sum(jnp.where(iota((1, 128), 1) == at, row, 0.0))


def second_kernel(place, live, s_ref, finv, tmap, resid, z_old, c_old, slots, sums, got, z_out, c_out, w_out, r_out, send):
    gamma = pick_lane(sums[0:1, :], 30)
    delta = pick_lane(sums[0:1, :], 31)
    alpha = gamma / delta
    w = meet(place, live, c_old, got)
    w_out[...] = w
    y = face_apply(finv, w) + prolong(tmap, coarse_values(slots, got))
    z = z_old[...] - alpha * y
    r = resid[...] - alpha * w
    z_out[...] = z
    r_out[...] = r
    image = subdomain_apply(s_ref, z)
    c_out[...] = image
    gamma_new = shared_dot(r, z)
    new_new = jnp.sum(sides(z) * image)
    old_new = jnp.sum(sides(z_old[...]) * image)
    new_old = jnp.sum(sides(z) * c_old[...])
    line = tag(
        jnp.zeros((1, 128), F32), (0, gamma_new), (1, new_new), (2, old_new), (3, new_old)
    )
    send[:, 0:128] = jnp.broadcast_to(line, (DEV, 128))
    send[:, 128:] = jnp.zeros((DEV, 512), F32)
    post(place, live, image, send)


def second(place, live, *rest):
    small = jax.ShapeDtypeStruct((8, NF), F32)
    return pl.pallas_call(
        second_kernel,
        in_specs=[smem(), smem()] + [vmem()] * 9,
        out_shape=[small, small, small, small, jax.ShapeDtypeStruct((DEV, 640), F32)],
        compiler_params=pltpu.CompilerParams(vmem_limit_bytes=14 * 2**20),
        cost_estimate=pl.CostEstimate(flops=10**7, transcendentals=0, bytes_accessed=12 * 2**20),
        name="second",
    )(place, live, *rest)


def last_kernel(place, live, z_old, w_old, z_new, c_new, resid, sums, got, x_out, r_out):
    line = jnp.sum(got[:, 0:128], axis=0, keepdims=True)
    gamma = pick_lane(sums[0:1, :], 30)
    delta = pick_lane(sums[0:1, :], 31)
    alpha = gamma / delta
    gamma_new = pick_lane(line, 0)
    beta = gamma_new / gamma
    curve = pick_lane(line, 1) + beta * (pick_lane(line, 2) + pick_lane(line, 3)) + beta * beta * delta
    alpha_new = gamma_new / curve
    w = meet(place, live, c_new[...], got)
    search = z_new[...] + beta * z_old[...]
    along = w + beta * w_old[...]
    x = sides(alpha * z_old[...] + alpha_new * search)
    r = sides(resid[...] - alpha_new * along)
    for s in range(2):
        x_out[s, 0] = x[4 * s : 4 * s + 4]
        r_out[s, 0] = r[4 * s : 4 * s + 4]


def last(place, live, *rest):
    out = jax.ShapeDtypeStruct((2, 1, 4, NF), F32)
    return pl.pallas_call(
        last_kernel,
        in_specs=[smem(), smem()] + [vmem()] * 7,
        out_shape=[out, out],
        compiler_params=pltpu.CompilerParams(vmem_limit_bytes=6 * 2**20),
        cost_estimate=pl.CostEstimate(flops=10**6, transcendentals=0, bytes_accessed=2**20),
        name="last",
    )(place, live, *rest)


def shift(value, axis, steps):
    count = lax.axis_size(axis)
    first_, last_ = max(0, -steps), min(count, count - steps)
    return lax.ppermute(value, axis, [(source, source + steps) for source in range(first_, last_)])


def exchange(packet):
    return lax.all_to_all(packet, GX_GY, 0, 0, tiled=True)


def shards(inverse, couple, stiff, basis, loads, order, corner_index, coarse_inverse):
    ix = lax.axis_index(GX)
    iy = lax.axis_index(GY)
    place = jnp.stack([ix, iy]).astype(jnp.int32)
    live = jnp.stack([ix > 0, ix < GRID_X - 1, iy > 0, iy < GRID_Y - 1]).astype(F32)
    s_full, p_in, p_n, p_s, p_w, p_e, t_n, t_s, t_w, t_e = schur(order, inverse, couple, stiff, basis, loads, corner_index)
    q_s = shift(t_n, GX, -1)
    q_n = shift(t_s, GX, 1)
    q_e = shift(t_w, GY, -1)
    q_w = shift(t_e, GY, 1)
    finv, tmap, resid, smooth, slots, send = faces(
        place, live, *(pltpu.with_memory_space_constraint(p, pltpu.HBM) for p in (p_in, p_n, p_s, p_w, p_e)), q_n, q_s, q_w, q_e
    )
    coarse, values = start(exchange(send), jnp.transpose(coarse_inverse))
    z0, c0, send = first(place, live, s_full, tmap, resid, smooth, slots, exchange(values))
    send, sums = owners(place, live, exchange(send), coarse, c0)
    z1, c1, w0, r1, send = second(place, live, s_full, finv, tmap, resid, z0, c0, slots, sums, exchange(send))
    return tuple(last(place, live, z0, w0, z1, c1, r1, sums, exchange(send)))


def solution(mesh):
    torus = Mesh(mesh.devices.reshape(4, 2, 4, 2, 2), GX_GY)
    in_specs = (
        P(GX, GY, None, None),
        P(GX, GY, None, None),
        P(GX, GY, None, None, None),
        P(GX, GY, None, None),
        P(GX, GY, None, None),
        P(GX, GY, None, None),
        P(GX, GY, None),
        P(None, GX_GY),
    )
    out_specs = (P(GX, GY, None, None), P(GX, GY, None, None))
    return jax.shard_map(shards, mesh=torus, in_specs=in_specs, out_specs=out_specs, check_vma=False)
```
